256 devices in a mesh: gx: 64 (over z, y, x_hi), gy: 4 (over x_lo, core).
Axes of the slice: x: 4 (x_hi: 2, x_lo: 2; x = x_hi * 2 + x_lo), y: 4, z: 8, core: 2. Of those that a mesh axis runs over, the one named last changes fastest.
Arguments:
- points: bfloat16 [4, 64, 64, 32, 128], P('gy', 'gx'), may hold values from -6 to 6
- counts: int32 [4, 64, 64], P('gy', 'gx'), may hold values from 10 to 32, as said below
- voxels: int32 [4, 64, 64, 32], P('gy', 'gx'), may hold values from 0 to 1023, as said below
- occupancy: int32 [64, 4, 2], P('gx', 'gy'), may hold values from 0 to 1, as said below
- weight: bfloat16 [27, 96, 96], replicated, may hold values from -0.125 to 0.125
- w_in: bfloat16 [128, 96], replicated, may hold values from -0.5 to 0.5
- cotangent: bfloat16 [512, 32, 16, 96], P('gx', 'gy'), may hold values from -6 to 6
Outputs:
- point_feat: bfloat16 [4, 64, 64, 32, 96], P('gy', 'gx')
- point_grad: bfloat16 [4, 64, 64, 32, 128], P('gy', 'gx')
- weight_grad: float32 [27, 96, 96], replicated
The draws below stay inside these ranges and needn't reach their ends.
Inputs may be any that keep to these rules, and one draw needn't show every extreme that they name: `counts`: in each gy row one owner receives 32 rows from every source. `voxels`: every slot's voxel lies in an occupied block of its owner tile. `occupancy`: every tile has at least one occupied block.
All inputs are finite; a program needn't handle non-finite values.
Results may differ from the reference program's by a relative error of at most 0.01.
Values may be sent and summed in bfloat16 or wider, within the bound.
A program may use at most 64 MiB of HBM per device.

```python
import jax
import jax.numpy as jnp
from jax import lax

C = 96
FEAT = 128
BZ = 2
CAP = 32
NX = 512
NY = 32
NZ = 16
N_GX = 64
N_GY = 4


def draw_counts(key, part):
    lowest = max(1, CAP // 3)
    base = jax.random.randint(key, (N_GY, N_GX, N_GX), lowest, CAP + 1)
    full = jax.random.randint(jax.random.fold_in(key, 7), (N_GY, 1, 1), 0, N_GX)
    column = lax.broadcasted_iota(jnp.int32, (N_GY, N_GX, N_GX), 2)
    return jnp.where(column == full, CAP, base).astype(jnp.int32)


def block_layout(key):
    base = jax.random.randint(jax.random.fold_in(key, 11), (N_GX, N_GY, BZ), 0, 3)
    occupied = (base < 2).astype(jnp.int32)
    forced = jax.random.randint(jax.random.fold_in(key, 13), (N_GX, N_GY, 1), 0, BZ)
    block_id = lax.broadcasted_iota(jnp.int32, (N_GX, N_GY, BZ), 2)
    return jnp.where(block_id == forced, 1, occupied).astype(jnp.int32)


def draw_occupancy(key, part):
    return block_layout(key)


def draw_voxels(key, part):
    occupied = jnp.transpose(block_layout(key), (1, 0, 2))
    total = jnp.sum(occupied, axis=-1)
    running = jnp.cumsum(occupied, axis=-1)
    shape_slots = (N_GY, N_GX, N_GX, CAP)
    picked = jax.random.randint(jax.random.fold_in(key, 17), shape_slots, 0, 4096) % total[:, None, :, None]
    match = (running[:, None, :, None, :] == picked[..., None] + 1) & (occupied[:, None, :, None, :] == 1)
    block_id = lax.broadcasted_iota(jnp.int32, shape_slots + (BZ,), 4)
    chosen = jnp.sum(jnp.where(match, block_id, 0), axis=-1)
    local = jax.random.randint(jax.random.fold_in(key, 19), shape_slots, 0, 512)
    inner_x = local // 64
    inner_y = local // 8 % 8
    inner_z = local % 8
    return ((inner_x * 8 + inner_y) * (8 * BZ) + chosen * 8 + inner_z).astype(jnp.int32)


def steps_of(own_key, extent, shards, least, high):
    def one(position, blocks):
        heights = jax.random.uniform(jax.random.fold_in(jax.random.fold_in(own_key, 6), position), (blocks,), jnp.float32, least / len(shards), high / len(shards))
        return jnp.repeat(jnp.exp(heights), extent[position] // blocks).reshape((-1,) + (1,) * (len(extent) - position - 1))

    factor_of = one(*shards[0])
    for cut in shards[1:]:
        factor_of = factor_of * one(*cut)
    return factor_of


def centred(stream_key, dims, scale, bound, split=(), held_as=jnp.bfloat16):
    result = scale * jax.random.normal(stream_key, dims, jnp.float32)
    if split:
        result = result * steps_of(stream_key, dims, split, -0.22, 0.18)
    return jnp.clip(result, -bound, bound).astype(held_as)


def setup_inputs(seed: int = 0) -> dict:
    streams_of = jax.random.split(jax.random.key(seed), 8)
    points = centred(streams_of[0], (N_GY, N_GX, N_GX, CAP, FEAT), 1.0, 6.0, ((0, 4), (1, 64)))
    counts = draw_counts(jax.random.fold_in(streams_of[7], 71), 0)
    voxels = draw_voxels(jax.random.fold_in(streams_of[7], 71), 0)
    occupancy = draw_occupancy(jax.random.fold_in(streams_of[7], 71), 0)
    weight = centred(streams_of[4], (27, C, C), (27 * C) ** -0.5, 0.125)
    w_in = centred(streams_of[5], (FEAT, C), FEAT ** -0.5, 0.5)
    cotangent = centred(streams_of[6], (NX, NY, NZ, C), 1.0, 6.0, ((0, 64), (1, 4)))
    return {"points": points, "counts": counts, "voxels": voxels, "occupancy": occupancy, "weight": weight, "w_in": w_in, "cotangent": cotangent}


def voxel_mask(occupancy):
    grown = jnp.repeat(jnp.repeat(jnp.repeat(occupancy, 8, axis=0), 8, axis=1), 8, axis=2)
    return grown.astype(jnp.float32)


def reference(points, counts, voxels, occupancy, weight, w_in, cotangent):
    nx_all = 8 * N_GX
    ny_all = 8 * N_GY
    nz_all = 8 * BZ
    slots = jax.lax.broadcasted_iota(jnp.int32, voxels.shape, 3)
    valid = (slots < counts[..., None]).astype(jnp.float32)
    proj = jnp.dot(points.reshape(-1, FEAT), w_in, preferred_element_type=jnp.float32)
    proj = (proj.reshape(voxels.shape + (C,)) * valid[..., None]).astype(jnp.bfloat16)
    rowid = jax.lax.broadcasted_iota(jnp.int32, voxels.shape, 0)
    owner = jax.lax.broadcasted_iota(jnp.int32, voxels.shape, 2)
    coord_x = owner * 8 + voxels // (8 * nz_all)
    coord_y = rowid * 8 + (voxels // nz_all) % 8
    coord_z = voxels % nz_all
    flat = ((coord_x * ny_all + coord_y) * nz_all + coord_z).astype(jnp.int32)
    mask = voxel_mask(occupancy)[..., None]
    f0 = jnp.zeros((nx_all * ny_all * nz_all, C), jnp.float32).at[flat.reshape(-1)].add(proj.reshape(-1, C).astype(jnp.float32))
    f0 = (f0.reshape(nx_all, ny_all, nz_all, C) * mask).astype(jnp.bfloat16)
    gm = (cotangent.astype(jnp.float32) * mask).astype(jnp.bfloat16)
    pad_f = jnp.pad(f0.astype(jnp.float32), ((1, 1), (1, 1), (1, 1), (0, 0)))
    pad_g = jnp.pad(gm.astype(jnp.float32), ((1, 1), (1, 1), (1, 1), (0, 0)))
    gm32 = gm.astype(jnp.float32)
    y = jnp.zeros((nx_all, ny_all, nz_all, C), jnp.float32)
    df0 = jnp.zeros((nx_all, ny_all, nz_all, C), jnp.float32)
    grads = []
    for tap in range(27):
        a, b, c = tap // 9, (tap // 3) % 3, tap % 3
        wt = weight[tap].astype(jnp.float32)
        window = pad_f[a:a + nx_all, b:b + ny_all, c:c + nz_all]
        y = y + jnp.einsum("xyzi,io->xyzo", window, wt)
        grads.append(jnp.einsum("xyzi,xyzo->io", window, gm32))
        back = pad_g[2 - a:2 - a + nx_all, 2 - b:2 - b + ny_all, 2 - c:2 - c + nz_all]
        df0 = df0 + jnp.einsum("xyzo,io->xyzi", back, wt)
    y = (y * mask).astype(jnp.bfloat16)
    df0 = (df0 * mask).astype(jnp.bfloat16)
    weight_grad = jnp.stack(grads)
    y_rows = y.reshape(-1, C)[flat]
    point_feat = (y_rows.astype(jnp.float32) * valid[..., None]).astype(jnp.bfloat16)
    d_rows = df0.reshape(-1, C)[flat].reshape(-1, C)
    pg = jnp.dot(d_rows, w_in.T, preferred_element_type=jnp.float32).reshape(voxels.shape + (FEAT,))
    point_grad = (pg * valid[..., None]).astype(jnp.bfloat16)
    return point_feat, point_grad, weight_grad
```

```python
import functools

import jax
import jax.numpy as jnp
from jax import lax
from jax.experimental import pallas as pl
from jax.experimental.pallas import tpu as pltpu
from jax.sharding import PartitionSpec as P

MESH = pl.DeviceIdType.MESH
F32 = jnp.float32
BF16 = jnp.bfloat16
C = 96
L = 128
CAP = 32
NV = 1024
SUB = 64


def dot(a, b):
    return jnp.dot(a, b, preferred_element_type=F32)


def dot_nt(a, b):
    return lax.dot_general(a, b, (((1,), (1,)), ((), ())), preferred_element_type=F32)


def kernel(
    ngx,
    ngy,
    pz,
    pts,
    vox,
    occ,
    weight,
    w_in,
    cot,
    feat_out,
    grad_out,
    wgrad_out,
    got_pts,
    got_vox,
    rows_d,
    rows_y,
    got_d,
    got_y,
    gpad,
    fpad,
    wf,
    wb,
    winp,
    wint,
    oht,
    field_d,
    field_y,
    wg,
    pk,
    rs_buf,
    z_buf,
    ag_buf,
    vox_s,
    vox_r,
    pts_s,
    pts_r,
    d_s,
    d_r,
    y_s,
    y_r,
    rs_s,
    rs_r,
    z_s,
    z_r,
    ag_s,
    ag_r,
    g_s,
    g_r,
    f_s,
    f_r,
):
    gx = lax.axis_index("gx")
    gy = lax.axis_index("gy")
    nz = ngx // pz
    plane = pz * ngy
    zi = gx // pz
    xy = lax.rem(gx, pz)
    slot = xy * ngy + gy
    rows = ngx * CAP

    gpad[...] = jnp.zeros_like(gpad)
    fpad[...] = jnp.zeros_like(fpad)

    barrier = pltpu.get_barrier_semaphore()

    def greet(px, py):
        pl.semaphore_signal(barrier, inc=1, device_id=(px, py), device_id_type=MESH)

    @pl.loop(1, ngx)
    def _(k):
        greet(lax.rem(gx + k, ngx), gy)

    @pl.loop(0, pz)
    def _(k):
        for m in range(1, ngy):
            greet(zi * pz + k, lax.rem(gy + m, ngy))

    directions = ((1, 0), (-1, 0), (0, 1), (0, -1), (1, 1), (1, -1), (-1, 1), (-1, -1))

    def exists(dx, dy):
        ok = jnp.bool_(True)
        if dx == 1:
            ok = ok & (gx < ngx - 1)
        if dx == -1:
            ok = ok & (gx > 0)
        if dy == 1:
            ok = ok & (gy < ngy - 1)
        if dy == -1:
            ok = ok & (gy > 0)
        return ok

    for dx, dy in directions[4:]:

        @pl.when(exists(dx, dy))
        def _():
            greet(gx + dx, gy + dy)

    o0 = occ[0].astype(F32)
    o1 = occ[1].astype(F32)

    @pl.loop(0, 8)
    def _(x):
        value = cot[x].astype(F32)
        z = lax.broadcasted_iota(jnp.int32, value.shape, 1)
        gpad[x + 1, pl.ds(1, 8), :, pl.ds(0, C)] = (value * jnp.where(z < 8, o0, o1)).astype(BF16)

    wf[...] = jnp.zeros_like(wf)
    wb[...] = jnp.zeros_like(wb)
    for tap in range(27):
        ab, c = tap // 3, tap % 3
        value = weight[tap]
        wf[ab * L : ab * L + C, c * L : c * L + C] = value
        wb[c * L : c * L + C, ab * L : ab * L + C] = value
    winp[...] = jnp.zeros_like(winp)
    winp[:, 0:C] = w_in[...]
    wint[...] = jnp.transpose(winp[...].astype(F32)).astype(BF16)

    corners = sum(
        (exists(dx, dy).astype(jnp.int32) for dx, dy in directions[4:]), jnp.int32(0)
    )
    pl.semaphore_wait(barrier, (ngx - 1) + pz * (ngy - 1) + corners)

    def exchange(src, dst, send, recv):
        @pl.loop(1, ngx)
        def _(k):
            peer = lax.rem(gx + k, ngx)
            pltpu.make_async_remote_copy(
                src_ref=src.at[peer],
                dst_ref=dst.at[gx],
                send_sem=send,
                recv_sem=recv,
                device_id=(peer, gy),
                device_id_type=MESH,
            ).start()

    def whole(ref, count, send, recv):
        part = ref.at[pl.ds(0, count)]
        return pltpu.make_async_remote_copy(
            src_ref=part,
            dst_ref=part,
            send_sem=send,
            recv_sem=recv,
            device_id=(gx, gy),
            device_id_type=MESH,
        )

    def halo(ref, d, send, recv):
        dx, dy = directions[d]

        def span(delta, edge):
            if delta == 0:
                return pl.ds(1, 8), pl.ds(1, 8)
            return (8, 0) if delta == 1 else (1, 9)

        sx, tx = span(dx, 0)
        sy, ty = span(dy, 0)
        return pltpu.make_async_remote_copy(
            src_ref=ref.at[sx, sy],
            dst_ref=ref.at[tx, ty],
            send_sem=send.at[d],
            recv_sem=recv.at[d],
            device_id=(gx + dx, gy + dy),
            device_id_type=MESH,
        )

    def halo_start(ref, send, recv):
        for d, (dx, dy) in enumerate(directions):

            @pl.when(exists(dx, dy))
            def _():
                halo(ref, d, send, recv).start()

    def halo_wait(ref, send, recv):
        for d, (dx, dy) in enumerate(directions):

            @pl.when(exists(-dx, -dy))
            def _():
                halo(ref, d, send, recv).wait_recv()

    def halo_sent(ref, send, recv):
        for d, (dx, dy) in enumerate(directions):

            @pl.when(exists(dx, dy))
            def _():
                halo(ref, d, send, recv).wait_send()

    exchange(vox, got_vox, vox_s, vox_r)
    halo_start(gpad, g_s, g_r)
    exchange(pts, got_pts, pts_s, pts_r)
    got_vox[gx] = vox[gx]
    got_pts[gx] = pts[gx]

    def lift(total, lower, upper):
        count = total.shape[0]
        z = lax.broadcasted_iota(jnp.int32, total.shape, 0) % 16
        down = pltpu.roll(lower, 1, 0)
        up = pltpu.roll(upper, count - 1, 0)
        total = total + jnp.where(z == 0, 0.0, down) + jnp.where(z == 15, 0.0, up)
        return total * jnp.where(z < 8, o0, o1)

    step = 4

    halo_wait(gpad, g_s, g_r)

    @pl.loop(0, 8 // step)
    def _(i):
        windows = [
            gpad[pl.ds(i * step + 2 - a, step), 2 - b : 10 - b].reshape(step * L, L)
            for a in range(3)
            for b in range(3)
        ]
        z3 = dot_nt(jnp.concatenate(windows, axis=1), wb[...])
        out = lift(z3[:, L : 2 * L], z3[:, 2 * L :], z3[:, :L])
        field_d[pl.ds(pl.multiple_of(i * step * L, step * L), step * L), :] = out.astype(BF16)

    whole(got_vox, ngx - 1, vox_s, vox_r).wait_recv()
    chunk = min(256, rows)
    ids = got_vox[...].reshape(ngx, L)
    high = (ids >> 5).astype(F32).astype(BF16)
    low = (ids & 31).astype(F32).astype(BF16)
    ones = jnp.ones((L, L), BF16)

    @pl.loop(0, rows // chunk)
    def _(i):
        owner = lax.broadcasted_iota(jnp.int32, (chunk, ngx), 0) // CAP + i * (chunk // CAP)
        pick = jnp.where(
            owner == lax.broadcasted_iota(jnp.int32, (chunk, ngx), 1), 1.0, 0.0
        ).astype(BF16)
        here = (
            lax.broadcasted_iota(jnp.int32, (chunk, L), 0) % CAP
            == lax.broadcasted_iota(jnp.int32, (chunk, L), 1)
        )
        hi = jnp.where(here, dot(pick, high) * 32.0, 0.0).astype(BF16)
        lo = jnp.where(here, dot(pick, low), 0.0).astype(BF16)
        wanted = dot(hi, ones) + dot(lo, ones)
        lane = lax.broadcasted_iota(jnp.int32, (chunk, L), 1).astype(F32)
        for j in range(NV // L):
            oht[pl.ds(pl.multiple_of(i * chunk, chunk), chunk), j * L : (j + 1) * L] = jnp.where(
                wanted == lane + float(j * L), 1.0, 0.0
            ).astype(BF16)

    group = min(512, rows)

    def gather(field, out):
        @pl.loop(0, rows // group)
        def _(i):
            got = dot(oht[pl.ds(pl.multiple_of(i * group, group), group), :], field[...])
            out[pl.ds(i * (group // CAP), group // CAP)] = got.astype(BF16).reshape(
                group // CAP, CAP, L
            )

    gather(field_d, rows_d)
    exchange(rows_d, got_d, d_s, d_r)
    got_d[gx] = rows_d[gx]

    whole(got_pts, ngx - 1, pts_s, pts_r).wait_recv()
    proj_t = dot_nt(wint[...], got_pts[...].reshape(rows, L)).astype(BF16)
    sum_t = dot(proj_t, oht[...])
    z_lane = lax.broadcasted_iota(jnp.int32, sum_t.shape, 1) % 16
    sum_t = (sum_t * jnp.where(z_lane < 8, o0, o1)).astype(BF16).astype(F32)
    f0 = jnp.transpose(sum_t).astype(BF16).reshape(8, 8, 16, L)
    fpad[1:9, 1:9] = f0
    halo_start(fpad, f_s, f_r)

    f_t = sum_t[:C]
    z_own = z_lane[:C]
    stack = jnp.concatenate(
        [
            jnp.where(z_own == 0, 0.0, pltpu.roll(f_t, 1, 1)),
            f_t,
            jnp.where(z_own == 15, 0.0, pltpu.roll(f_t, NV - 1, 1)),
        ],
        axis=0,
    ).astype(BF16)
    for ab in range(9):
        a, b = ab // 3, ab % 3
        window = gpad[2 - a : 10 - a, 2 - b : 10 - b].reshape(NV, L)
        wg[:, ab * L : (ab + 1) * L] = dot(stack, window)

    def tap_block(tap):
        ab, c = tap // 3, tap % 3
        return wg[c * C : (c + 1) * C, ab * L : (ab + 1) * L]

    lane = lax.broadcasted_iota(jnp.int32, (C, L), 1)
    for g in range(7):
        last = tap_block(4 * g + 3) if g < 6 else jnp.zeros((C, L), F32)
        for j in range(3):
            extra = pltpu.roll(last, C - 32 * j, 1)
            block = jnp.where(lane < C, tap_block(4 * g + j), extra)
            pk[9 * g + 3 * j : 9 * g + 3 * j + 3] = block.astype(BF16).reshape(3, CAP, L)
    pk[63] = jnp.zeros((CAP, L), BF16)

    sub = SUB // plane

    @pl.loop(1, plane)
    def _(k):
        peer = lax.rem(slot + k, plane)
        pltpu.make_async_remote_copy(
            src_ref=pk.at[pl.ds(peer * sub, sub)],
            dst_ref=rs_buf.at[slot],
            send_sem=rs_s,
            recv_sem=rs_r,
            device_id=(zi * pz + peer // ngy, lax.rem(peer, ngy)),
            device_id_type=MESH,
        ).start()

    rs_buf[slot] = pk[pl.ds(slot * sub, sub)]

    halo_wait(fpad, f_s, f_r)

    @pl.loop(0, 8 // step)
    def _(i):
        windows = [
            fpad[pl.ds(i * step + a, step), b : b + 8].reshape(step * L, L)
            for a in range(3)
            for b in range(3)
        ]
        z3 = dot(jnp.concatenate(windows, axis=1), wf[...])
        out = lift(z3[:, L : 2 * L], z3[:, :L], z3[:, 2 * L :])
        field_y[pl.ds(pl.multiple_of(i * step * L, step * L), step * L), :] = out.astype(BF16)

    gather(field_y, rows_y)
    exchange(rows_y, got_y, y_s, y_r)
    got_y[gx] = rows_y[gx]

    whole(rs_buf, plane - 1, rs_s, rs_r).wait_recv()
    total = rs_buf[0].astype(F32)
    for k in range(1, plane):
        total = total + rs_buf[k].astype(F32)
    z_buf[zi] = total.astype(BF16)

    @pl.loop(1, nz)
    def _(k):
        peer = lax.rem(zi + k, nz)
        pltpu.make_async_remote_copy(
            src_ref=z_buf.at[zi],
            dst_ref=z_buf.at[zi],
            send_sem=z_s,
            recv_sem=z_r,
            device_id=(peer * pz + xy, gy),
            device_id_type=MESH,
        ).start()

    whole(got_d, ngx - 1, d_s, d_r).wait_recv()

    @pl.loop(0, rows // group)
    def _(i):
        part = pl.ds(i * (group // CAP), group // CAP)
        got = dot_nt(got_d[part].reshape(group, L), winp[...])
        grad_out[part] = got.astype(BF16).reshape(group // CAP, CAP, L)

    whole(z_buf, nz - 1, z_s, z_r).wait_recv()
    total = z_buf[0].astype(F32)
    for k in range(1, nz):
        total = total + z_buf[k].astype(F32)
    ag_buf[slot] = total.astype(BF16)

    @pl.loop(1, plane)
    def _(k):
        peer = lax.rem(slot + k, plane)
        pltpu.make_async_remote_copy(
            src_ref=ag_buf.at[slot],
            dst_ref=ag_buf.at[slot],
            send_sem=ag_s,
            recv_sem=ag_r,
            device_id=(zi * pz + peer // ngy, lax.rem(peer, ngy)),
            device_id_type=MESH,
        ).start()

    whole(got_y, ngx - 1, y_s, y_r).wait_recv()
    feat_out[...] = got_y[:, :, 0:C]

    whole(ag_buf, plane - 1, ag_s, ag_r).wait_recv()
    summed = ag_buf[...].reshape(SUB, CAP, L)
    for g in range(7):
        blocks = [
            summed[9 * g + 3 * j : 9 * g + 3 * j + 3].reshape(C, L).astype(F32) for j in range(3)
        ]
        for j in range(3):
            wgrad_out[4 * g + j] = blocks[j][:, :C]
        if g < 6:
            last = pltpu.roll(blocks[0], 32, 1)
            for j in (1, 2):
                moved = pltpu.roll(blocks[j], 32 + 32 * j, 1)
                last = jnp.where(lane >= 32 * j, moved, last)
            wgrad_out[4 * g + 3] = last[:, :C]

    whole(vox, ngx - 1, vox_s, vox_r).wait_send()
    whole(pts, ngx - 1, pts_s, pts_r).wait_send()
    whole(rows_d, ngx - 1, d_s, d_r).wait_send()
    whole(rows_y, ngx - 1, y_s, y_r).wait_send()
    whole(rs_buf, plane - 1, rs_s, rs_r).wait_send()
    whole(z_buf, nz - 1, z_s, z_r).wait_send()
    whole(ag_buf, plane - 1, ag_s, ag_r).wait_send()
    halo_sent(gpad, g_s, g_r)
    halo_sent(fpad, f_s, f_r)


def on_device(ngx, ngy, pz, points, counts, voxels, occupancy, weight, w_in, cotangent):
    slots = lax.broadcasted_iota(jnp.int32, (ngx, CAP), 1)
    used = jnp.where(slots < counts[0, 0][:, None], voxels[0, 0], -32)
    used = jnp.pad(used, ((0, 0), (0, L - CAP))).reshape(ngx, 1, L)
    rows = ngx * CAP
    nz = ngx // pz
    plane = pz * ngy
    vmem = pl.BlockSpec(memory_space=pltpu.VMEM)
    dma = pltpu.SemaphoreType.DMA
    feat, grad, wgrad = pl.pallas_call(
        functools.partial(kernel, ngx, ngy, pz),
        out_shape=(
            jax.ShapeDtypeStruct((ngx, CAP, C), BF16),
            jax.ShapeDtypeStruct((ngx, CAP, L), BF16),
            jax.ShapeDtypeStruct((27, C, C), F32),
        ),
        in_specs=[vmem, vmem, pl.BlockSpec(memory_space=pltpu.SMEM), vmem, vmem, vmem],
        out_specs=(vmem, vmem, vmem),
        scratch_shapes=[
            pltpu.VMEM((ngx, CAP, L), BF16),
            pltpu.VMEM((ngx, 1, L), jnp.int32),
            pltpu.VMEM((ngx, CAP, L), BF16),
            pltpu.VMEM((ngx, CAP, L), BF16),
            pltpu.VMEM((ngx, CAP, L), BF16),
            pltpu.VMEM((ngx, CAP, L), BF16),
            pltpu.VMEM((10, 10, 16, L), BF16),
            pltpu.VMEM((10, 10, 16, L), BF16),
            pltpu.VMEM((9 * L, 3 * L), BF16),
            pltpu.VMEM((3 * L, 9 * L), BF16),
            pltpu.VMEM((L, L), BF16),
            pltpu.VMEM((L, L), BF16),
            pltpu.VMEM((rows, NV), BF16),
            pltpu.VMEM((NV, L), BF16),
            pltpu.VMEM((NV, L), BF16),
            pltpu.VMEM((3 * C, 9 * L), F32),
            pltpu.VMEM((SUB, CAP, L), BF16),
            pltpu.VMEM((plane, SUB // plane, CAP, L), BF16),
            pltpu.VMEM((nz, SUB // plane, CAP, L), BF16),
            pltpu.VMEM((plane, SUB // plane, CAP, L), BF16),
        ]
        + [dma] * 14
        + [dma((8,))] * 4,
        compiler_params=pltpu.CompilerParams(
            collective_id=0, has_side_effects=True, vmem_limit_bytes=56 * 1024 * 1024
        ),
    )(
        points.reshape(ngx, CAP, L),
        used,
        occupancy.reshape(2),
        weight,
        w_in,
        cotangent,
    )
    return feat[None, None], grad[None, None], wgrad


def solution(mesh):
    ngx, ngy = mesh.shape["gx"], mesh.shape["gy"]
    pz = ngx // 8
    placed = (
        P("gy", "gx", None, None, None),
        P("gy", "gx", None),
        P("gy", "gx", None, None),
        P("gx", "gy", None),
        P(),
        P(),
        P("gx", "gy", None, None),
    )
    return jax.shard_map(
        functools.partial(on_device, ngx, ngy, pz),
        mesh=mesh,
        in_specs=placed,
        out_specs=(P("gy", "gx", None, None, None), P("gy", "gx", None, None, None), P()),
        check_vma=False,
    )
```

```python
import functools

import jax
import jax.numpy as jnp
from jax import lax
from jax.experimental import pallas as pl
from jax.experimental.pallas import tpu as pltpu
from jax.sharding import PartitionSpec as P

MESH = pl.DeviceIdType.MESH
F32 = jnp.float32
BF16 = jnp.bfloat16
C = 96
L = 128
CAP = 32
NV = 1024
SUB = 64
PACK = CAP * C // L


def dot(a, b):
    return jnp.dot(a, b, preferred_element_type=F32)


def dot_nt(a, b):
    return lax.dot_general(a, b, (((1,), (1,)), ((), ())), preferred_element_type=F32)


def pack(value, owners):
    tiles = value.reshape(owners, 4, 8, L)
    tail = tiles[:, 3].reshape(owners * 8, L)
    lane = lax.broadcasted_iota(jnp.int32, (owners * 8, L), 1)
    parts = [
        jnp.where(
            lane < C, tiles[:, j].reshape(owners * 8, L), pltpu.roll(tail, C - 32 * j, 1)
        ).reshape(owners, 1, 8, L)
        for j in range(3)
    ]
    return jnp.concatenate(parts, axis=1).reshape(owners, PACK, L)


def unpack(value, owners):
    tiles = value.reshape(owners, 3, 8, L)
    lane = lax.broadcasted_iota(jnp.int32, (owners * 8, L), 1)
    parts = [tiles[:, j].reshape(owners * 8, L) for j in range(3)]
    tail = jnp.zeros((owners * 8, L), value.dtype)
    for j in range(3):
        moved = pltpu.roll(parts[j], 32 + 32 * j, 1)
        tail = jnp.where((lane >= 32 * j) & (lane < 32 * j + 32), moved, tail)
    parts = [jnp.where(lane < C, part, 0.0) for part in parts] + [tail]
    return jnp.concatenate([part.reshape(owners, 1, 8, L) for part in parts], axis=1).reshape(
        owners * CAP, L
    )


def kernel(
    ngx,
    ngy,
    pz,
    pts,
    voxels_t,
    counts,
    occ,
    weight,
    w_in_t,
    cot,
    got_y,
    got_d,
    ag_buf,
    vox,
    rows_p,
    got_p,
    proj,
    got_vox,
    rows_d,
    rows_y,
    gpad,
    fpad,
    wf,
    wb,
    wint,
    oht,
    field_d,
    field_y,
    wg,
    pk,
    rs_buf,
    z_buf,
    vox_s,
    vox_r,
    pts_s,
    pts_r,
    d_s,
    d_r,
    y_s,
    y_r,
    rs_s,
    rs_r,
    z_s,
    z_r,
    ag_s,
    ag_r,
    g_s,
    g_r,
    f_s,
    f_r,
):
    gx = lax.axis_index("gx")
    gy = lax.axis_index("gy")
    nz = ngx // pz
    plane = pz * ngy
    zi = gx // pz
    xy = lax.rem(gx, pz)
    slot = xy * ngy + gy
    rows = ngx * CAP

    gpad[...] = jnp.zeros_like(gpad)
    fpad[...] = jnp.zeros_like(fpad)

    barrier = pltpu.get_barrier_semaphore()

    def greet(px, py):
        pl.semaphore_signal(barrier, inc=1, device_id=(px, py), device_id_type=MESH)

    @pl.loop(1, ngx)
    def _(k):
        greet(lax.rem(gx + k, ngx), gy)

    @pl.loop(0, pz)
    def _(k):
        for m in range(1, ngy):
            greet(zi * pz + k, lax.rem(gy + m, ngy))

    directions = ((1, 0), (-1, 0), (0, 1), (0, -1), (1, 1), (1, -1), (-1, 1), (-1, -1))

    def exists(dx, dy):
        ok = jnp.bool_(True)
        if dx == 1:
            ok = ok & (gx < ngx - 1)
        if dx == -1:
            ok = ok & (gx > 0)
        if dy == 1:
            ok = ok & (gy < ngy - 1)
        if dy == -1:
            ok = ok & (gy > 0)
        return ok

    for dx, dy in directions[4:]:

        @pl.when(exists(dx, dy))
        def _():
            greet(gx + dx, gy + dy)

    used = jnp.where(
        lax.broadcasted_iota(jnp.int32, (CAP, ngx), 0) < counts[...], voxels_t[...], -32
    ).astype(F32)
    used = jnp.concatenate([used, jnp.zeros((L - CAP, ngx), F32)], axis=0)
    if ngx < L:
        used = jnp.concatenate([used, jnp.zeros((L, L - ngx), F32)], axis=1)
    vox[...] = jnp.transpose(used)[:ngx].astype(jnp.int32).reshape(ngx, 1, L)

    o0 = occ[0].astype(F32)
    o1 = occ[1].astype(F32)

    @pl.loop(0, 8)
    def _(x):
        value = cot[x].astype(F32)
        z = lax.broadcasted_iota(jnp.int32, value.shape, 1)
        gpad[x + 1, pl.ds(1, 8), :, pl.ds(0, C)] = (value * jnp.where(z < 8, o0, o1)).astype(BF16)

    wf[...] = jnp.zeros_like(wf)
    wb[...] = jnp.zeros_like(wb)
    for tap in range(27):
        ab, c = tap // 3, tap % 3
        value = weight[tap]
        wf[ab * L : ab * L + C, c * L : c * L + C] = value
        wb[c * L : c * L + C, ab * L : ab * L + C] = value
    wint[...] = jnp.zeros_like(wint)
    wint[0:C, :] = w_in_t[...]

    group = min(512, rows)
    own = group // CAP

    @pl.loop(0, rows // group)
    def _(i):
        part = pl.ds(i * own, own)
        value = dot_nt(pts[part].reshape(group, L), wint[...])
        rows_p[part] = pack(value, own).astype(BF16)


    corners = sum(
        (exists(dx, dy).astype(jnp.int32) for dx, dy in directions[4:]), jnp.int32(0)
    )
    pl.semaphore_wait(barrier, (ngx - 1) + pz * (ngy - 1) + corners)

    def exchange(src, dst, send, recv):
        @pl.loop(1, ngx)
        def _(k):
            peer = lax.rem(gx + k, ngx)
            pltpu.make_async_remote_copy(
                src_ref=src.at[peer],
                dst_ref=dst.at[gx],
                send_sem=send,
                recv_sem=recv,
                device_id=(peer, gy),
                device_id_type=MESH,
            ).start()

    def whole(ref, count, send, recv):
        part = ref.at[pl.ds(0, count)]
        return pltpu.make_async_remote_copy(
            src_ref=part,
            dst_ref=part,
            send_sem=send,
            recv_sem=recv,
            device_id=(gx, gy),
            device_id_type=MESH,
        )

    def halo(ref, d, send, recv):
        dx, dy = directions[d]

        def span(delta, edge):
            if delta == 0:
                return pl.ds(1, 8), pl.ds(1, 8)
            return (8, 0) if delta == 1 else (1, 9)

        sx, tx = span(dx, 0)
        sy, ty = span(dy, 0)
        return pltpu.make_async_remote_copy(
            src_ref=ref.at[sx, sy],
            dst_ref=ref.at[tx, ty],
            send_sem=send.at[d],
            recv_sem=recv.at[d],
            device_id=(gx + dx, gy + dy),
            device_id_type=MESH,
        )

    def halo_start(ref, send, recv):
        for d, (dx, dy) in enumerate(directions):

            @pl.when(exists(dx, dy))
            def _():
                halo(ref, d, send, recv).start()

    def halo_wait(ref, send, recv):
        for d, (dx, dy) in enumerate(directions):

            @pl.when(exists(-dx, -dy))
            def _():
                halo(ref, d, send, recv).wait_recv()

    def halo_sent(ref, send, recv):
        for d, (dx, dy) in enumerate(directions):

            @pl.when(exists(dx, dy))
            def _():
                halo(ref, d, send, recv).wait_send()

    exchange(vox, got_vox, vox_s, vox_r)
    halo_start(gpad, g_s, g_r)
    exchange(rows_p, got_p, pts_s, pts_r)
    got_vox[gx] = vox[gx]
    got_p[gx] = rows_p[gx]

    def lift(total, lower, upper):
        count = total.shape[0]
        z = lax.broadcasted_iota(jnp.int32, total.shape, 0) % 16
        down = pltpu.roll(lower, 1, 0)
        up = pltpu.roll(upper, count - 1, 0)
        total = total + jnp.where(z == 0, 0.0, down) + jnp.where(z == 15, 0.0, up)
        return total * jnp.where(z < 8, o0, o1)

    step = 4

    halo_wait(gpad, g_s, g_r)

    @pl.loop(0, 8 // step)
    def _(i):
        windows = [
            gpad[pl.ds(i * step + 2 - a, step), 2 - b : 10 - b].reshape(step * L, L)
            for a in range(3)
            for b in range(3)
        ]
        z3 = dot_nt(jnp.concatenate(windows, axis=1), wb[...])
        out = lift(z3[:, L : 2 * L], z3[:, 2 * L :], z3[:, :L])
        field_d[pl.ds(pl.multiple_of(i * step * L, step * L), step * L), :] = out.astype(BF16)

    whole(got_vox, ngx - 1, vox_s, vox_r).wait_recv()
    chunk = min(256, rows)
    ids = got_vox[...].reshape(ngx, L)
    high = (ids >> 5).astype(F32).astype(BF16)
    low = (ids & 31).astype(F32).astype(BF16)
    ones = jnp.ones((L, L), BF16)

    @pl.loop(0, rows // chunk)
    def _(i):
        owner = lax.broadcasted_iota(jnp.int32, (chunk, ngx), 0) // CAP + i * (chunk // CAP)
        pick = jnp.where(
            owner == lax.broadcasted_iota(jnp.int32, (chunk, ngx), 1), 1.0, 0.0
        ).astype(BF16)
        here = (
            lax.broadcasted_iota(jnp.int32, (chunk, L), 0) % CAP
            == lax.broadcasted_iota(jnp.int32, (chunk, L), 1)
        )
        hi = jnp.where(here, dot(pick, high) * 32.0, 0.0).astype(BF16)
        lo = jnp.where(here, dot(pick, low), 0.0).astype(BF16)
        wanted = dot(hi, ones) + dot(lo, ones)
        lane = lax.broadcasted_iota(jnp.int32, (chunk, L), 1).astype(F32)
        for j in range(NV // L):
            oht[pl.ds(pl.multiple_of(i * chunk, chunk), chunk), j * L : (j + 1) * L] = jnp.where(
                wanted == lane + float(j * L), 1.0, 0.0
            ).astype(BF16)

    def gather(field, out):
        @pl.loop(0, rows // group)
        def _(i):
            got = dot(oht[pl.ds(pl.multiple_of(i * group, group), group), :], field[...])
            out[pl.ds(i * own, own)] = pack(got, own).astype(BF16)

    gather(field_d, rows_d)

    whole(got_p, ngx - 1, pts_s, pts_r).wait_recv()

    @pl.loop(0, rows // group)
    def _(i):
        value = unpack(got_p[pl.ds(i * own, own)].astype(F32), own)
        proj[pl.ds(pl.multiple_of(i * group, group), group), :] = value.astype(BF16)

    eye = jnp.where(
        lax.broadcasted_iota(jnp.int32, (L, L), 0) == lax.broadcasted_iota(jnp.int32, (L, L), 1),
        1.0,
        0.0,
    ).astype(BF16)
    proj_t = dot_nt(eye, proj[...]).astype(BF16)
    sum_t = dot(proj_t, oht[...])
    z_lane = lax.broadcasted_iota(jnp.int32, sum_t.shape, 1) % 16
    sum_t = (sum_t * jnp.where(z_lane < 8, o0, o1)).astype(BF16).astype(F32)
    f0 = jnp.transpose(sum_t).astype(BF16).reshape(8, 8, 16, L)
    fpad[1:9, 1:9] = f0
    halo_start(fpad, f_s, f_r)

    f_t = sum_t[:C]
    z_own = z_lane[:C]
    stack = jnp.concatenate(
        [
            jnp.where(z_own == 0, 0.0, pltpu.roll(f_t, 1, 1)),
            f_t,
            jnp.where(z_own == 15, 0.0, pltpu.roll(f_t, NV - 1, 1)),
        ],
        axis=0,
    ).astype(BF16)
    for ab in range(9):
        a, b = ab // 3, ab % 3
        window = gpad[2 - a : 10 - a, 2 - b : 10 - b].reshape(NV, L)
        wg[:, ab * L : (ab + 1) * L] = dot(stack, window)

    def tap_block(tap):
        ab, c = tap // 3, tap % 3
        return wg[c * C : (c + 1) * C, ab * L : (ab + 1) * L]

    lane = lax.broadcasted_iota(jnp.int32, (C, L), 1)
    for g in range(7):
        last = tap_block(4 * g + 3) if g < 6 else jnp.zeros((C, L), F32)
        for j in range(3):
            extra = pltpu.roll(last, C - 32 * j, 1)
            block = jnp.where(lane < C, tap_block(4 * g + j), extra)
            pk[9 * g + 3 * j : 9 * g + 3 * j + 3] = block.astype(BF16).reshape(3, CAP, L)
    pk[63] = jnp.zeros((CAP, L), BF16)

    sub = SUB // plane

    @pl.loop(1, plane)
    def _(k):
        peer = lax.rem(slot + k, plane)
        pltpu.make_async_remote_copy(
            src_ref=pk.at[pl.ds(peer * sub, sub)],
            dst_ref=rs_buf.at[slot],
            send_sem=rs_s,
            recv_sem=rs_r,
            device_id=(zi * pz + peer // ngy, lax.rem(peer, ngy)),
            device_id_type=MESH,
        ).start()

    rs_buf[slot] = pk[pl.ds(slot * sub, sub)]
    exchange(rows_d, got_d, d_s, d_r)
    got_d[gx] = rows_d[gx]

    halo_wait(fpad, f_s, f_r)

    @pl.loop(0, 8 // step)
    def _(i):
        windows = [
            fpad[pl.ds(i * step + a, step), b : b + 8].reshape(step * L, L)
            for a in range(3)
            for b in range(3)
        ]
        z3 = dot(jnp.concatenate(windows, axis=1), wf[...])
        out = lift(z3[:, L : 2 * L], z3[:, :L], z3[:, 2 * L :])
        field_y[pl.ds(pl.multiple_of(i * step * L, step * L), step * L), :] = out.astype(BF16)

    gather(field_y, rows_y)
    exchange(rows_y, got_y, y_s, y_r)
    got_y[gx] = rows_y[gx]

    whole(rs_buf, plane - 1, rs_s, rs_r).wait_recv()
    total = rs_buf[0].astype(F32)
    for k in range(1, plane):
        total = total + rs_buf[k].astype(F32)
    z_buf[zi] = total.astype(BF16)

    @pl.loop(1, nz)
    def _(k):
        peer = lax.rem(zi + k, nz)
        pltpu.make_async_remote_copy(
            src_ref=z_buf.at[zi],
            dst_ref=z_buf.at[zi],
            send_sem=z_s,
            recv_sem=z_r,
            device_id=(peer * pz + xy, gy),
            device_id_type=MESH,
        ).start()

    whole(z_buf, nz - 1, z_s, z_r).wait_recv()
    total = z_buf[0].astype(F32)
    for k in range(1, nz):
        total = total + z_buf[k].astype(F32)
    ag_buf[slot] = total.astype(BF16)

    @pl.loop(1, plane)
    def _(k):
        peer = lax.rem(slot + k, plane)
        pltpu.make_async_remote_copy(
            src_ref=ag_buf.at[slot],
            dst_ref=ag_buf.at[slot],
            send_sem=ag_s,
            recv_sem=ag_r,
            device_id=(zi * pz + peer // ngy, lax.rem(peer, ngy)),
            device_id_type=MESH,
        ).start()

    whole(got_d, ngx - 1, d_s, d_r).wait_recv()
    whole(got_y, ngx - 1, y_s, y_r).wait_recv()
    whole(ag_buf, plane - 1, ag_s, ag_r).wait_recv()

    whole(vox, ngx - 1, vox_s, vox_r).wait_send()
    whole(rows_p, ngx - 1, pts_s, pts_r).wait_send()
    whole(rows_d, ngx - 1, d_s, d_r).wait_send()
    whole(rows_y, ngx - 1, y_s, y_r).wait_send()
    whole(rs_buf, plane - 1, rs_s, rs_r).wait_send()
    whole(z_buf, nz - 1, z_s, z_r).wait_send()
    whole(ag_buf, plane - 1, ag_s, ag_r).wait_send()
    halo_sent(gpad, g_s, g_r)
    halo_sent(fpad, f_s, f_r)


def finish(own, got_y, got_d, summed, w_in_t, feat_out, grad_out, wgrad_out):
    step = pl.program_id(0)
    part = pl.ds(jnp.minimum(step, got_y.shape[0] // own - 1) * own, own)
    feat = unpack(got_y[part].astype(F32), own).astype(BF16)
    feat_out[...] = feat[:, :C].reshape(own, CAP, C)
    grad = unpack(got_d[part].astype(F32), own)[:, :C].astype(BF16)
    grad_out[...] = dot(grad, w_in_t[...]).astype(BF16).reshape(own, CAP, L)

    lane = lax.broadcasted_iota(jnp.int32, (C, L), 1)
    first = 9 * jnp.minimum(step, 6)
    sub = summed.shape[1]
    blocks = [
        jnp.concatenate(
            [summed[(first + r) // sub, lax.rem(first + r, sub)] for r in range(3 * j, 3 * j + 3)]
        ).astype(F32)
        for j in range(3)
    ]
    for j in range(3):
        wgrad_out[j] = blocks[j][:, :C]
    last = pltpu.roll(blocks[0], 32, 1)
    for j in (1, 2):
        moved = pltpu.roll(blocks[j], 32 + 32 * j, 1)
        last = jnp.where(lane >= 32 * j, moved, last)
    wgrad_out[3] = last[:, :C]


def on_device(ngx, ngy, pz, points, counts, voxels, occupancy, weight, w_in, cotangent):
    rows = ngx * CAP
    nz = ngx // pz
    plane = pz * ngy
    vmem = pl.BlockSpec(memory_space=pltpu.VMEM)
    dma = pltpu.SemaphoreType.DMA
    got_y, got_d, summed = pl.pallas_call(
        functools.partial(kernel, ngx, ngy, pz),
        out_shape=(
            pltpu.VMEM((ngx, PACK, L), BF16),
            pltpu.VMEM((ngx, PACK, L), BF16),
            pltpu.VMEM((plane, SUB // plane, CAP, L), BF16),
        ),
        in_specs=[vmem, vmem, vmem, pl.BlockSpec(memory_space=pltpu.SMEM), vmem, vmem, vmem],
        out_specs=(vmem, vmem, vmem),
        scratch_shapes=[
            pltpu.VMEM((ngx, 1, L), jnp.int32),
            pltpu.VMEM((ngx, PACK, L), BF16),
            pltpu.VMEM((ngx, PACK, L), BF16),
            pltpu.VMEM((rows, L), BF16),
            pltpu.VMEM((ngx, 1, L), jnp.int32),
            pltpu.VMEM((ngx, PACK, L), BF16),
            pltpu.VMEM((ngx, PACK, L), BF16),
            pltpu.VMEM((10, 10, 16, L), BF16),
            pltpu.VMEM((10, 10, 16, L), BF16),
            pltpu.VMEM((9 * L, 3 * L), BF16),
            pltpu.VMEM((3 * L, 9 * L), BF16),
            pltpu.VMEM((L, L), BF16),
            pltpu.VMEM((rows, NV), BF16),
            pltpu.VMEM((NV, L), BF16),
            pltpu.VMEM((NV, L), BF16),
            pltpu.VMEM((3 * C, 9 * L), F32),
            pltpu.VMEM((SUB, CAP, L), BF16),
            pltpu.VMEM((plane, SUB // plane, CAP, L), BF16),
            pltpu.VMEM((nz, SUB // plane, CAP, L), BF16),
        ]
        + [dma] * 14
        + [dma((8,))] * 4,
        compiler_params=pltpu.CompilerParams(
            collective_id=0, has_side_effects=True, vmem_limit_bytes=56 * 1024 * 1024
        ),
    )(
        points.reshape(ngx, CAP, L),
        voxels.reshape(ngx, CAP).T,
        counts.reshape(1, ngx),
        occupancy.reshape(2),
        weight,
        w_in.T,
        cotangent,
    )
    steps = 8
    own = pl.cdiv(ngx, steps)
    last = ngx // own - 1
    feat, grad, wgrad = pl.pallas_call(
        functools.partial(finish, own),
        grid=(steps,),
        out_shape=(
            jax.ShapeDtypeStruct((ngx, CAP, C), BF16),
            jax.ShapeDtypeStruct((ngx, CAP, L), BF16),
            jax.ShapeDtypeStruct((27, C, C), F32),
        ),
        in_specs=[vmem, vmem, vmem, vmem],
        out_specs=(
            pl.BlockSpec((own, CAP, C), lambda i: (jnp.minimum(i, last), 0, 0)),
            pl.BlockSpec((own, CAP, L), lambda i: (jnp.minimum(i, last), 0, 0)),
            pl.BlockSpec((4, C, C), lambda i: (jnp.minimum(i, 6), 0, 0)),
        ),
    )(
        *(pltpu.with_memory_space_constraint(x, pltpu.VMEM) for x in (got_y, got_d, summed)),
        w_in.T,
    )
    return feat[None, None], grad[None, None], wgrad


def solution(mesh):
    ngx, ngy = mesh.shape["gx"], mesh.shape["gy"]
    pz = ngx // 8
    placed = (
        P("gy", "gx", None, None, None),
        P("gy", "gx", None),
        P("gy", "gx", None, None),
        P("gx", "gy", None),
        P(),
        P(),
        P("gx", "gy", None, None),
    )
    return jax.shard_map(
        functools.partial(on_device, ngx, ngy, pz),
        mesh=mesh,
        in_specs=placed,
        out_specs=(P("gy", "gx", None, None, None), P("gy", "gx", None, None, None), P()),
        check_vma=False,
    )
```

```python
import functools

import jax
import jax.numpy as jnp
from jax import lax
from jax.experimental import pallas as pl
from jax.experimental.pallas import tpu as pltpu
from jax.sharding import PartitionSpec as P

MESH = pl.DeviceIdType.MESH
F32 = jnp.float32
BF16 = jnp.bfloat16
C = 96
L = 128
CAP = 32
NV = 1024
SUB = 64
PACK = CAP * C // L


def dot(a, b):
    return jnp.dot(a, b, preferred_element_type=F32)


def dot_nt(a, b):
    return lax.dot_general(a, b, (((1,), (1,)), ((), ())), preferred_element_type=F32)


def pack(value, owners):
    tiles = value.reshape(owners, 4, 8, L)
    tail = tiles[:, 3].reshape(owners * 8, L)
    lane = lax.broadcasted_iota(jnp.int32, (owners * 8, L), 1)
    parts = [
        jnp.where(
            lane < C, tiles[:, j].reshape(owners * 8, L), pltpu.roll(tail, C - 32 * j, 1)
        ).reshape(owners, 1, 8, L)
        for j in range(3)
    ]
    return jnp.concatenate(parts, axis=1).reshape(owners, PACK, L)


def unpack(value, owners):
    tiles = value.reshape(owners, 3, 8, L)
    lane = lax.broadcasted_iota(jnp.int32, (owners * 8, L), 1)
    parts = [tiles[:, j].reshape(owners * 8, L) for j in range(3)]
    tail = jnp.zeros((owners * 8, L), value.dtype)
    for j in range(3):
        moved = pltpu.roll(parts[j], 32 + 32 * j, 1)
        tail = jnp.where((lane >= 32 * j) & (lane < 32 * j + 32), moved, tail)
    parts = [jnp.where(lane < C, part, 0.0) for part in parts] + [tail]
    return jnp.concatenate([part.reshape(owners, 1, 8, L) for part in parts], axis=1).reshape(
        owners * CAP, L
    )


def kernel(
    ngx,
    ngy,
    pz,
    pts_in,
    voxels_in,
    counts_in,
    occ,
    weight_in,
    w_in_t,
    cot_in,
    feat,
    grad,
    ag_buf,
    pts,
    voxels_t,
    counts,
    weight,
    cot,
    in_sem,
    got_y,
    got_d,
    vox,
    rows_p,
    got_p,
    proj,
    got_vox,
    rows_d,
    rows_y,
    gpad,
    fpad,
    wf,
    wb,
    wint,
    oht,
    field_d,
    field_y,
    wg,
    pk,
    rs_buf,
    z_buf,
    vox_s,
    vox_r,
    pts_s,
    pts_r,
    d_s,
    d_r,
    y_s,
    y_r,
    rs_s,
    rs_r,
    z_s,
    z_r,
    ag_s,
    ag_r,
    g_s,
    g_r,
    f_s,
    f_r,
):
    gx = lax.axis_index("gx")
    gy = lax.axis_index("gy")
    nz = ngx // pz
    plane = pz * ngy
    zi = gx // pz
    xy = lax.rem(gx, pz)
    slot = xy * ngy + gy
    rows = ngx * CAP

    wint[C:L, :] = jnp.zeros((L - C, L), BF16)
    fetches = [
        pltpu.make_async_copy(src, dst, in_sem.at[n])
        for n, (src, dst) in enumerate(
            (
                (voxels_in, voxels_t),
                (counts_in, counts),
                (cot_in, cot),
                (w_in_t, wint.at[pl.ds(0, C)]),
                (pts_in, pts),
                (weight_in, weight),
            )
        )
    ]
    for fetch in fetches:
        fetch.start()
    gpad[...] = jnp.zeros_like(gpad)
    fpad[...] = jnp.zeros_like(fpad)

    barrier = pltpu.get_barrier_semaphore()

    def greet(px, py):
        pl.semaphore_signal(barrier, inc=1, device_id=(px, py), device_id_type=MESH)

    @pl.loop(1, ngx)
    def _(k):
        greet(lax.rem(gx + k, ngx), gy)

    @pl.loop(0, pz)
    def _(k):
        for m in range(1, ngy):
            greet(zi * pz + k, lax.rem(gy + m, ngy))

    directions = ((1, 0), (-1, 0), (0, 1), (0, -1), (1, 1), (1, -1), (-1, 1), (-1, -1))

    def exists(dx, dy):
        ok = jnp.bool_(True)
        if dx == 1:
            ok = ok & (gx < ngx - 1)
        if dx == -1:
            ok = ok & (gx > 0)
        if dy == 1:
            ok = ok & (gy < ngy - 1)
        if dy == -1:
            ok = ok & (gy > 0)
        return ok

    for dx, dy in directions[4:]:

        @pl.when(exists(dx, dy))
        def _():
            greet(gx + dx, gy + dy)

    fetches[0].wait()
    fetches[1].wait()
    used = jnp.where(
        lax.broadcasted_iota(jnp.int32, (CAP, ngx), 0) < counts[...], voxels_t[...], -32
    ).astype(F32)
    used = jnp.concatenate([used, jnp.zeros((L - CAP, ngx), F32)], axis=0)
    if ngx < L:
        used = jnp.concatenate([used, jnp.zeros((L, L - ngx), F32)], axis=1)
    vox[...] = jnp.transpose(used)[:ngx].astype(jnp.int32).reshape(ngx, 1, L)

    fetches[2].wait()
    o0 = occ[0].astype(F32)
    o1 = occ[1].astype(F32)

    @pl.loop(0, 8)
    def _(x):
        value = cot[x].astype(F32)
        z = lax.broadcasted_iota(jnp.int32, value.shape, 1)
        gpad[x + 1, pl.ds(1, 8), :, pl.ds(0, C)] = (value * jnp.where(z < 8, o0, o1)).astype(BF16)

    corners = sum(
        (exists(dx, dy).astype(jnp.int32) for dx, dy in directions[4:]), jnp.int32(0)
    )
    pl.semaphore_wait(barrier, (ngx - 1) + pz * (ngy - 1) + corners)

    group = min(512, rows)
    own = group // CAP
    groups = ngx // own

    def base_of(i):
        return lax.rem(gx // own + i, groups) * own

    def exchange_group(src, dst, send, recv, base):
        @pl.loop(0, own)
        def _(k):
            peer = base + lax.rem(gx + k, own)

            @pl.when(peer != gx)
            def _():
                pltpu.make_async_remote_copy(
                    src_ref=src.at[peer],
                    dst_ref=dst.at[gx],
                    send_sem=send,
                    recv_sem=recv,
                    device_id=(peer, gy),
                    device_id_type=MESH,
                ).start()

    def exchange(src, dst, send, recv):
        @pl.loop(1, ngx)
        def _(k):
            peer = lax.rem(gx + k, ngx)
            pltpu.make_async_remote_copy(
                src_ref=src.at[peer],
                dst_ref=dst.at[gx],
                send_sem=send,
                recv_sem=recv,
                device_id=(peer, gy),
                device_id_type=MESH,
            ).start()

    def whole(ref, count, send, recv):
        part = ref.at[pl.ds(0, count)]
        return pltpu.make_async_remote_copy(
            src_ref=part,
            dst_ref=part,
            send_sem=send,
            recv_sem=recv,
            device_id=(gx, gy),
            device_id_type=MESH,
        )

    def halo(ref, d, send, recv):
        dx, dy = directions[d]

        def span(delta, edge):
            if delta == 0:
                return pl.ds(1, 8), pl.ds(1, 8)
            return (8, 0) if delta == 1 else (1, 9)

        sx, tx = span(dx, 0)
        sy, ty = span(dy, 0)
        return pltpu.make_async_remote_copy(
            src_ref=ref.at[sx, sy],
            dst_ref=ref.at[tx, ty],
            send_sem=send.at[d],
            recv_sem=recv.at[d],
            device_id=(gx + dx, gy + dy),
            device_id_type=MESH,
        )

    def halo_start(ref, send, recv):
        for d, (dx, dy) in enumerate(directions):

            @pl.when(exists(dx, dy))
            def _():
                halo(ref, d, send, recv).start()

    def halo_wait(ref, send, recv):
        for d, (dx, dy) in enumerate(directions):

            @pl.when(exists(-dx, -dy))
            def _():
                halo(ref, d, send, recv).wait_recv()

    def halo_sent(ref, send, recv):
        for d, (dx, dy) in enumerate(directions):

            @pl.when(exists(dx, dy))
            def _():
                halo(ref, d, send, recv).wait_send()

    exchange(vox, got_vox, vox_s, vox_r)
    halo_start(gpad, g_s, g_r)
    fetches[3].wait()
    fetches[4].wait()

    @pl.loop(0, groups)
    def _(i):
        base = base_of(i)
        part = pl.ds(base, own)
        rows_p[part] = pack(dot_nt(pts[part].reshape(group, L), wint[...]), own).astype(BF16)
        exchange_group(rows_p, got_p, pts_s, pts_r, base)

    got_vox[gx] = vox[gx]
    got_p[gx] = rows_p[gx]

    fetches[5].wait()
    wf[...] = jnp.zeros_like(wf)
    wb[...] = jnp.zeros_like(wb)
    for tap in range(27):
        ab, c = tap // 3, tap % 3
        value = weight[tap]
        wf[ab * L : ab * L + C, c * L : c * L + C] = value
        wb[c * L : c * L + C, ab * L : ab * L + C] = value

    def lift(total, lower, upper):
        count = total.shape[0]
        z = lax.broadcasted_iota(jnp.int32, total.shape, 0) % 16
        down = pltpu.roll(lower, 1, 0)
        up = pltpu.roll(upper, count - 1, 0)
        total = total + jnp.where(z == 0, 0.0, down) + jnp.where(z == 15, 0.0, up)
        return total * jnp.where(z < 8, o0, o1)

    step = 4

    halo_wait(gpad, g_s, g_r)

    @pl.loop(0, 8 // step)
    def _(i):
        windows = [
            gpad[pl.ds(i * step + 2 - a, step), 2 - b : 10 - b].reshape(step * L, L)
            for a in range(3)
            for b in range(3)
        ]
        z3 = dot_nt(jnp.concatenate(windows, axis=1), wb[...])
        out = lift(z3[:, L : 2 * L], z3[:, 2 * L :], z3[:, :L])
        field_d[pl.ds(pl.multiple_of(i * step * L, step * L), step * L), :] = out.astype(BF16)

    whole(got_vox, ngx - 1, vox_s, vox_r).wait_recv()
    chunk = min(256, rows)
    ids = got_vox[...].reshape(ngx, L)
    high = (ids >> 5).astype(F32).astype(BF16)
    low = (ids & 31).astype(F32).astype(BF16)
    ones = jnp.ones((L, L), BF16)

    @pl.loop(0, rows // chunk)
    def _(i):
        owner = lax.broadcasted_iota(jnp.int32, (chunk, ngx), 0) // CAP + i * (chunk // CAP)
        pick = jnp.where(
            owner == lax.broadcasted_iota(jnp.int32, (chunk, ngx), 1), 1.0, 0.0
        ).astype(BF16)
        here = (
            lax.broadcasted_iota(jnp.int32, (chunk, L), 0) % CAP
            == lax.broadcasted_iota(jnp.int32, (chunk, L), 1)
        )
        hi = jnp.where(here, dot(pick, high) * 32.0, 0.0).astype(BF16)
        lo = jnp.where(here, dot(pick, low), 0.0).astype(BF16)
        wanted = dot(hi, ones) + dot(lo, ones)
        lane = lax.broadcasted_iota(jnp.int32, (chunk, L), 1).astype(F32)
        for j in range(NV // L):
            oht[pl.ds(pl.multiple_of(i * chunk, chunk), chunk), j * L : (j + 1) * L] = jnp.where(
                wanted == lane + float(j * L), 1.0, 0.0
            ).astype(BF16)

    def gather(field, out, base):
        at = pl.ds(pl.multiple_of(base * CAP, group), group)
        out[pl.ds(base, own)] = pack(dot(oht[at, :], field[...]), own).astype(BF16)

    @pl.loop(0, groups)
    def _(i):
        gather(field_d, rows_d, i * own)


    whole(got_p, ngx - 1, pts_s, pts_r).wait_recv()

    @pl.loop(0, rows // group)
    def _(i):
        value = unpack(got_p[pl.ds(i * own, own)].astype(F32), own)
        proj[pl.ds(pl.multiple_of(i * group, group), group), :] = value.astype(BF16)

    eye = jnp.where(
        lax.broadcasted_iota(jnp.int32, (L, L), 0) == lax.broadcasted_iota(jnp.int32, (L, L), 1),
        1.0,
        0.0,
    ).astype(BF16)
    proj_t = dot_nt(eye, proj[...]).astype(BF16)
    sum_t = dot(proj_t, oht[...])
    z_lane = lax.broadcasted_iota(jnp.int32, sum_t.shape, 1) % 16
    sum_t = (sum_t * jnp.where(z_lane < 8, o0, o1)).astype(BF16).astype(F32)
    f0 = jnp.transpose(sum_t).astype(BF16).reshape(8, 8, 16, L)
    fpad[1:9, 1:9] = f0
    halo_start(fpad, f_s, f_r)

    f_t = sum_t[:C]
    z_own = z_lane[:C]
    stack = jnp.concatenate(
        [
            jnp.where(z_own == 0, 0.0, pltpu.roll(f_t, 1, 1)),
            f_t,
            jnp.where(z_own == 15, 0.0, pltpu.roll(f_t, NV - 1, 1)),
        ],
        axis=0,
    ).astype(BF16)
    for ab in range(9):
        a, b = ab // 3, ab % 3
        window = gpad[2 - a : 10 - a, 2 - b : 10 - b].reshape(NV, L)
        wg[:, ab * L : (ab + 1) * L] = dot(stack, window)

    def tap_block(tap):
        ab, c = tap // 3, tap % 3
        return wg[c * C : (c + 1) * C, ab * L : (ab + 1) * L]

    lane = lax.broadcasted_iota(jnp.int32, (C, L), 1)
    for g in range(7):
        last = tap_block(4 * g + 3) if g < 6 else jnp.zeros((C, L), F32)
        for j in range(3):
            extra = pltpu.roll(last, C - 32 * j, 1)
            block = jnp.where(lane < C, tap_block(4 * g + j), extra)
            pk[9 * g + 3 * j : 9 * g + 3 * j + 3] = block.astype(BF16).reshape(3, CAP, L)
    pk[63] = jnp.zeros((CAP, L), BF16)

    sub = SUB // plane

    @pl.loop(1, plane)
    def _(k):
        peer = lax.rem(slot + k, plane)
        pltpu.make_async_remote_copy(
            src_ref=pk.at[pl.ds(peer * sub, sub)],
            dst_ref=rs_buf.at[slot],
            send_sem=rs_s,
            recv_sem=rs_r,
            device_id=(zi * pz + peer // ngy, lax.rem(peer, ngy)),
            device_id_type=MESH,
        ).start()

    rs_buf[slot] = pk[pl.ds(slot * sub, sub)]
    exchange(rows_d, got_d, d_s, d_r)
    got_d[gx] = rows_d[gx]

    halo_wait(fpad, f_s, f_r)

    @pl.loop(0, 8 // step)
    def _(i):
        windows = [
            fpad[pl.ds(i * step + a, step), b : b + 8].reshape(step * L, L)
            for a in range(3)
            for b in range(3)
        ]
        z3 = dot(jnp.concatenate(windows, axis=1), wf[...])
        out = lift(z3[:, L : 2 * L], z3[:, :L], z3[:, 2 * L :])
        field_y[pl.ds(pl.multiple_of(i * step * L, step * L), step * L), :] = out.astype(BF16)

    whole(rs_buf, plane - 1, rs_s, rs_r).wait_recv()
    total = rs_buf[0].astype(F32)
    for k in range(1, plane):
        total = total + rs_buf[k].astype(F32)
    z_buf[zi] = total.astype(BF16)

    @pl.loop(1, nz)
    def _(k):
        peer = lax.rem(zi + k, nz)
        pltpu.make_async_remote_copy(
            src_ref=z_buf.at[zi],
            dst_ref=z_buf.at[zi],
            send_sem=z_s,
            recv_sem=z_r,
            device_id=(peer * pz + xy, gy),
            device_id_type=MESH,
        ).start()

    @pl.loop(0, groups)
    def _(i):
        base = base_of(i)
        gather(field_y, rows_y, base)
        exchange_group(rows_y, got_y, y_s, y_r, base)

    got_y[gx] = rows_y[gx]

    whole(z_buf, nz - 1, z_s, z_r).wait_recv()
    total = z_buf[0].astype(F32)
    for k in range(1, nz):
        total = total + z_buf[k].astype(F32)
    ag_buf[slot] = total.astype(BF16)

    @pl.loop(1, plane)
    def _(k):
        peer = lax.rem(slot + k, plane)
        pltpu.make_async_remote_copy(
            src_ref=ag_buf.at[slot],
            dst_ref=ag_buf.at[slot],
            send_sem=ag_s,
            recv_sem=ag_r,
            device_id=(zi * pz + peer // ngy, lax.rem(peer, ngy)),
            device_id_type=MESH,
        ).start()

    whole(got_d, ngx - 1, d_s, d_r).wait_recv()

    @pl.loop(0, groups)
    def _(i):
        part = pl.ds(i * own, own)
        value = unpack(got_d[part].astype(F32), own).astype(BF16)
        grad[part] = dot(value, wint[...]).astype(BF16).reshape(own, CAP, L)

    whole(got_y, ngx - 1, y_s, y_r).wait_recv()

    @pl.loop(0, groups)
    def _(i):
        part = pl.ds(i * own, own)
        value = unpack(got_y[part].astype(F32), own).astype(BF16)
        feat[part] = value[:, :C].reshape(own, CAP, C)

    whole(ag_buf, plane - 1, ag_s, ag_r).wait_recv()

    whole(vox, ngx - 1, vox_s, vox_r).wait_send()
    whole(rows_p, ngx - 1, pts_s, pts_r).wait_send()
    whole(rows_d, ngx - 1, d_s, d_r).wait_send()
    whole(rows_y, ngx - 1, y_s, y_r).wait_send()
    whole(rs_buf, plane - 1, rs_s, rs_r).wait_send()
    whole(z_buf, nz - 1, z_s, z_r).wait_send()
    whole(ag_buf, plane - 1, ag_s, ag_r).wait_send()
    halo_sent(gpad, g_s, g_r)
    halo_sent(fpad, f_s, f_r)


def finish(feat, grad, summed, feat_out, grad_out, wgrad_out, wgrad, sem):
    copies = [
        pltpu.make_async_copy(src, dst, sem.at[n])
        for n, (src, dst) in enumerate(((feat, feat_out), (grad, grad_out)))
    ]
    for copy in copies:
        copy.start()
    sub = summed.shape[1]
    lane = lax.broadcasted_iota(jnp.int32, (C, L), 1)
    for g in range(7):
        blocks = []
        for j in range(3):
            first = 9 * g + 3 * j
            parts = [summed[r // sub, r % sub] for r in range(first, first + 3)]
            blocks.append(jnp.concatenate(parts).astype(F32))
            wgrad[4 * g + j] = blocks[j][:, :C]
        count = 3
        if g < 6:
            last = pltpu.roll(blocks[0], 32, 1)
            for j in (1, 2):
                last = jnp.where(lane >= 32 * j, pltpu.roll(blocks[j], 32 + 32 * j, 1), last)
            wgrad[4 * g + 3] = last[:, :C]
            count = 4
        part = pl.ds(4 * g, count)
        copies.append(pltpu.make_async_copy(wgrad.at[part], wgrad_out.at[part], sem.at[2 + g]))
        copies[-1].start()
    for copy in copies:
        copy.wait()


def on_device(ngx, ngy, pz, points, counts, voxels, occupancy, weight, w_in, cotangent):
    rows = ngx * CAP
    nz = ngx // pz
    plane = pz * ngy
    vmem = pl.BlockSpec(memory_space=pltpu.VMEM)
    place = pl.BlockSpec(memory_space=pl.ANY)
    dma = pltpu.SemaphoreType.DMA
    feat, grad, summed = pl.pallas_call(
        functools.partial(kernel, ngx, ngy, pz),
        out_shape=(
            pltpu.VMEM((ngx, CAP, C), BF16),
            pltpu.VMEM((ngx, CAP, L), BF16),
            pltpu.VMEM((plane, SUB // plane, CAP, L), BF16),
        ),
        in_specs=[place, place, place, pl.BlockSpec(memory_space=pltpu.SMEM), place, place, place],
        out_specs=(vmem, vmem, vmem),
        scratch_shapes=[
            pltpu.VMEM((ngx, CAP, L), BF16),
            pltpu.VMEM((CAP, ngx), jnp.int32),
            pltpu.VMEM((1, ngx), jnp.int32),
            pltpu.VMEM((27, C, C), BF16),
            pltpu.VMEM((8, 8, 16, C), BF16),
            dma((6,)),
            pltpu.VMEM((ngx, PACK, L), BF16),
            pltpu.VMEM((ngx, PACK, L), BF16),
            pltpu.VMEM((ngx, 1, L), jnp.int32),
            pltpu.VMEM((ngx, PACK, L), BF16),
            pltpu.VMEM((ngx, PACK, L), BF16),
            pltpu.VMEM((rows, L), BF16),
            pltpu.VMEM((ngx, 1, L), jnp.int32),
            pltpu.VMEM((ngx, PACK, L), BF16),
            pltpu.VMEM((ngx, PACK, L), BF16),
            pltpu.VMEM((10, 10, 16, L), BF16),
            pltpu.VMEM((10, 10, 16, L), BF16),
            pltpu.VMEM((9 * L, 3 * L), BF16),
            pltpu.VMEM((3 * L, 9 * L), BF16),
            pltpu.VMEM((L, L), BF16),
            pltpu.VMEM((rows, NV), BF16),
            pltpu.VMEM((NV, L), BF16),
            pltpu.VMEM((NV, L), BF16),
            pltpu.VMEM((3 * C, 9 * L), F32),
            pltpu.VMEM((SUB, CAP, L), BF16),
            pltpu.VMEM((plane, SUB // plane, CAP, L), BF16),
            pltpu.VMEM((nz, SUB // plane, CAP, L), BF16),
        ]
        + [dma] * 14
        + [dma((8,))] * 4,
        compiler_params=pltpu.CompilerParams(
            collective_id=0, has_side_effects=True, vmem_limit_bytes=56 * 1024 * 1024
        ),
    )(
        points.reshape(ngx, CAP, L),
        voxels.reshape(ngx, CAP).T,
        counts.reshape(1, ngx),
        occupancy.reshape(2),
        weight,
        w_in.T,
        cotangent,
    )
    return_shape = (
        jax.ShapeDtypeStruct((ngx, CAP, C), BF16),
        jax.ShapeDtypeStruct((ngx, CAP, L), BF16),
        jax.ShapeDtypeStruct((27, C, C), F32),
    )
    feat, grad, wgrad = pl.pallas_call(
        finish,
        out_shape=return_shape,
        in_specs=[vmem, vmem, vmem],
        out_specs=(place, place, place),
        scratch_shapes=[pltpu.VMEM((27, C, C), F32), dma((9,))],
    )(*(pltpu.with_memory_space_constraint(x, pltpu.VMEM) for x in (feat, grad, summed)))
    return feat[None, None], grad[None, None], wgrad


def solution(mesh):
    ngx, ngy = mesh.shape["gx"], mesh.shape["gy"]
    pz = ngx // 8
    placed = (
        P("gy", "gx", None, None, None),
        P("gy", "gx", None),
        P("gy", "gx", None, None),
        P("gx", "gy", None),
        P(),
        P(),
        P("gx", "gy", None, None),
    )
    return jax.shard_map(
        functools.partial(on_device, ngx, ngy, pz),
        mesh=mesh,
        in_specs=placed,
        out_specs=(P("gy", "gx", None, None, None), P("gy", "gx", None, None, None), P()),
        check_vma=False,
    )
```

```python
import functools

import jax
import jax.numpy as jnp
from jax import lax
from jax.experimental import pallas as pl
from jax.experimental.pallas import tpu as pltpu
from jax.sharding import PartitionSpec as P

MESH = pl.DeviceIdType.MESH
F32 = jnp.float32
BF16 = jnp.bfloat16
C = 96
L = 128
CAP = 32
NV = 1024
SUB = 64
PACK = CAP * C // L


def dot(a, b):
    return jnp.dot(a, b, preferred_element_type=F32)


def dot_nt(a, b):
    return lax.dot_general(a, b, (((1,), (1,)), ((), ())), preferred_element_type=F32)


def pack(value, owners):
    tiles = value.reshape(owners, 4, 8, L)
    tail = tiles[:, 3].reshape(owners * 8, L)
    lane = lax.broadcasted_iota(jnp.int32, (owners * 8, L), 1)
    parts = [
        jnp.where(
            lane < C, tiles[:, j].reshape(owners * 8, L), pltpu.roll(tail, C - 32 * j, 1)
        ).reshape(owners, 1, 8, L)
        for j in range(3)
    ]
    return jnp.concatenate(parts, axis=1).reshape(owners, PACK, L)


def unpack(value, owners):
    tiles = value.reshape(owners, 3, 8, L)
    lane = lax.broadcasted_iota(jnp.int32, (owners * 8, L), 1)
    parts = [tiles[:, j].reshape(owners * 8, L) for j in range(3)]
    tail = jnp.zeros((owners * 8, L), value.dtype)
    for j in range(3):
        moved = pltpu.roll(parts[j], 32 + 32 * j, 1)
        tail = jnp.where((lane >= 32 * j) & (lane < 32 * j + 32), moved, tail)
    parts = [jnp.where(lane < C, part, 0.0) for part in parts] + [tail]
    return jnp.concatenate([part.reshape(owners, 1, 8, L) for part in parts], axis=1).reshape(
        owners * CAP, L
    )


def kernel(
    ngx,
    ngy,
    pz,
    pts_in,
    voxels_in,
    counts_in,
    occ,
    weight_in,
    w_in_t,
    cot_in,
    feat,
    grad,
    ag_buf,
    pts,
    voxels_t,
    counts,
    weight,
    cot,
    in_sem,
    got_y,
    got_d,
    vox,
    rows_p,
    got_p,
    proj,
    got_vox,
    rows_d,
    rows_y,
    gpad,
    fpad,
    wf,
    wb,
    wint,
    oht,
    field_d,
    field_y,
    wg,
    pk,
    pair_buf,
    rs_src,
    rs_buf,
    z_buf,
    vox_s,
    vox_r,
    pts_s,
    pts_r,
    d_s,
    d_r,
    y_s,
    y_r,
    rs_s,
    rs_r,
    z_s,
    z_r,
    ag_s,
    ag_r,
    g_s,
    g_r,
    f_s,
    f_r,
    pair_s,
    pair_r,
    swap_s,
    swap_r,
):
    gx = lax.axis_index("gx")
    gy = lax.axis_index("gy")
    nz = ngx // pz
    half = SUB // 2
    lanes = ngy // 2
    plane = pz * lanes
    zi = gx // pz
    xy = lax.rem(gx, pz)
    core = lax.rem(gy, 2)
    slot = xy * lanes + gy // 2
    rows = ngx * CAP

    wint[C:L, :] = jnp.zeros((L - C, L), BF16)
    fetches = [
        pltpu.make_async_copy(src, dst, in_sem.at[n])
        for n, (src, dst) in enumerate(
            (
                (voxels_in, voxels_t),
                (counts_in, counts),
                (cot_in, cot),
                (w_in_t, wint.at[pl.ds(0, C)]),
                (pts_in, pts),
                (weight_in, weight),
            )
        )
    ]
    for fetch in fetches:
        fetch.start()
    gpad[...] = jnp.zeros_like(gpad)
    fpad[...] = jnp.zeros_like(fpad)

    barrier = pltpu.get_barrier_semaphore()

    def greet(px, py):
        pl.semaphore_signal(barrier, inc=1, device_id=(px, py), device_id_type=MESH)

    @pl.loop(1, ngx)
    def _(k):
        greet(lax.rem(gx + k, ngx), gy)

    @pl.loop(0, pz)
    def _(k):
        for m in range(1, ngy):
            greet(zi * pz + k, lax.rem(gy + m, ngy))

    directions = ((1, 0), (-1, 0), (0, 1), (0, -1), (1, 1), (1, -1), (-1, 1), (-1, -1))

    def exists(dx, dy):
        ok = jnp.bool_(True)
        if dx == 1:
            ok = ok & (gx < ngx - 1)
        if dx == -1:
            ok = ok & (gx > 0)
        if dy == 1:
            ok = ok & (gy < ngy - 1)
        if dy == -1:
            ok = ok & (gy > 0)
        return ok

    for dx, dy in directions[4:]:

        @pl.when(exists(dx, dy))
        def _():
            greet(gx + dx, gy + dy)

    fetches[0].wait()
    fetches[1].wait()
    used = jnp.where(
        lax.broadcasted_iota(jnp.int32, (CAP, ngx), 0) < counts[...], voxels_t[...], -32
    ).astype(F32)
    used = jnp.concatenate([used, jnp.zeros((L - CAP, ngx), F32)], axis=0)
    if ngx < L:
        used = jnp.concatenate([used, jnp.zeros((L, L - ngx), F32)], axis=1)
    vox[...] = jnp.transpose(used)[:ngx].astype(jnp.int32).reshape(ngx, 1, L)

    fetches[2].wait()
    o0 = occ[0].astype(F32)
    o1 = occ[1].astype(F32)

    @pl.loop(0, 8)
    def _(x):
        value = cot[x].astype(F32)
        z = lax.broadcasted_iota(jnp.int32, value.shape, 1)
        gpad[x + 1, pl.ds(1, 8), :, pl.ds(0, C)] = (value * jnp.where(z < 8, o0, o1)).astype(BF16)

    corners = sum(
        (exists(dx, dy).astype(jnp.int32) for dx, dy in directions[4:]), jnp.int32(0)
    )
    pl.semaphore_wait(barrier, (ngx - 1) + pz * (ngy - 1) + corners)

    group = min(512, rows)
    own = group // CAP
    groups = ngx // own

    def base_of(i):
        return lax.rem(gx // own + i, groups) * own

    def exchange_group(src, dst, send, recv, base):
        @pl.loop(0, own)
        def _(k):
            peer = base + lax.rem(gx + k, own)

            @pl.when(peer != gx)
            def _():
                pltpu.make_async_remote_copy(
                    src_ref=src.at[peer],
                    dst_ref=dst.at[gx],
                    send_sem=send,
                    recv_sem=recv,
                    device_id=(peer, gy),
                    device_id_type=MESH,
                ).start()

    def exchange(src, dst, send, recv):
        @pl.loop(1, ngx)
        def _(k):
            peer = lax.rem(gx + k, ngx)
            pltpu.make_async_remote_copy(
                src_ref=src.at[peer],
                dst_ref=dst.at[gx],
                send_sem=send,
                recv_sem=recv,
                device_id=(peer, gy),
                device_id_type=MESH,
            ).start()

    def whole(ref, count, send, recv):
        part = ref.at[pl.ds(0, count)]
        return pltpu.make_async_remote_copy(
            src_ref=part,
            dst_ref=part,
            send_sem=send,
            recv_sem=recv,
            device_id=(gx, gy),
            device_id_type=MESH,
        )

    def halo(ref, d, send, recv):
        dx, dy = directions[d]

        def span(delta, edge):
            if delta == 0:
                return pl.ds(1, 8), pl.ds(1, 8)
            return (8, 0) if delta == 1 else (1, 9)

        sx, tx = span(dx, 0)
        sy, ty = span(dy, 0)
        return pltpu.make_async_remote_copy(
            src_ref=ref.at[sx, sy],
            dst_ref=ref.at[tx, ty],
            send_sem=send.at[d],
            recv_sem=recv.at[d],
            device_id=(gx + dx, gy + dy),
            device_id_type=MESH,
        )

    def halo_start(ref, send, recv):
        for d, (dx, dy) in enumerate(directions):

            @pl.when(exists(dx, dy))
            def _():
                halo(ref, d, send, recv).start()

    def halo_wait(ref, send, recv):
        for d, (dx, dy) in enumerate(directions):

            @pl.when(exists(-dx, -dy))
            def _():
                halo(ref, d, send, recv).wait_recv()

    def halo_sent(ref, send, recv):
        for d, (dx, dy) in enumerate(directions):

            @pl.when(exists(dx, dy))
            def _():
                halo(ref, d, send, recv).wait_send()

    exchange(vox, got_vox, vox_s, vox_r)
    halo_start(gpad, g_s, g_r)
    fetches[3].wait()
    fetches[4].wait()

    @pl.loop(0, groups)
    def _(i):
        base = base_of(i)
        part = pl.ds(base, own)
        rows_p[part] = pack(dot_nt(pts[part].reshape(group, L), wint[...]), own).astype(BF16)

    exchange(rows_p, got_p, pts_s, pts_r)
    got_vox[gx] = vox[gx]
    got_p[gx] = rows_p[gx]

    fetches[5].wait()
    wf[...] = jnp.zeros_like(wf)
    wb[...] = jnp.zeros_like(wb)
    for tap in range(27):
        ab, c = tap // 3, tap % 3
        value = weight[tap]
        wf[ab * L : ab * L + C, c * L : c * L + C] = value
        wb[c * L : c * L + C, ab * L : ab * L + C] = value

    def lift(total, lower, upper):
        count = total.shape[0]
        z = lax.broadcasted_iota(jnp.int32, total.shape, 0) % 16
        down = pltpu.roll(lower, 1, 0)
        up = pltpu.roll(upper, count - 1, 0)
        total = total + jnp.where(z == 0, 0.0, down) + jnp.where(z == 15, 0.0, up)
        return total * jnp.where(z < 8, o0, o1)

    step = 4

    halo_wait(gpad, g_s, g_r)

    @pl.loop(0, 8 // step)
    def _(i):
        windows = [
            gpad[pl.ds(i * step + 2 - a, step), 2 - b : 10 - b].reshape(step * L, L)
            for a in range(3)
            for b in range(3)
        ]
        z3 = dot_nt(jnp.concatenate(windows, axis=1), wb[...])
        out = lift(z3[:, L : 2 * L], z3[:, 2 * L :], z3[:, :L])
        field_d[pl.ds(pl.multiple_of(i * step * L, step * L), step * L), :] = out.astype(BF16)

    whole(got_vox, ngx - 1, vox_s, vox_r).wait_recv()
    chunk = min(256, rows)
    ids = got_vox[...].reshape(ngx, L)
    high = (ids >> 5).astype(F32).astype(BF16)
    low = (ids & 31).astype(F32).astype(BF16)
    ones = jnp.ones((L, L), BF16)

    @pl.loop(0, rows // chunk)
    def _(i):
        owner = lax.broadcasted_iota(jnp.int32, (chunk, ngx), 0) // CAP + i * (chunk // CAP)
        pick = jnp.where(
            owner == lax.broadcasted_iota(jnp.int32, (chunk, ngx), 1), 1.0, 0.0
        ).astype(BF16)
        here = (
            lax.broadcasted_iota(jnp.int32, (chunk, L), 0) % CAP
            == lax.broadcasted_iota(jnp.int32, (chunk, L), 1)
        )
        hi = jnp.where(here, dot(pick, high) * 32.0, 0.0).astype(BF16)
        lo = jnp.where(here, dot(pick, low), 0.0).astype(BF16)
        wanted = dot(hi, ones) + dot(lo, ones)
        lane = lax.broadcasted_iota(jnp.int32, (chunk, L), 1).astype(F32)
        for j in range(NV // L):
            oht[pl.ds(pl.multiple_of(i * chunk, chunk), chunk), j * L : (j + 1) * L] = jnp.where(
                wanted == lane + float(j * L), 1.0, 0.0
            ).astype(BF16)

    def gather(field, out, base):
        at = pl.ds(pl.multiple_of(base * CAP, group), group)
        out[pl.ds(base, own)] = pack(dot(oht[at, :], field[...]), own).astype(BF16)

    @pl.loop(0, groups)
    def _(i):
        gather(field_d, rows_d, i * own)


    whole(got_p, ngx - 1, pts_s, pts_r).wait_recv()

    @pl.loop(0, rows // group)
    def _(i):
        value = unpack(got_p[pl.ds(i * own, own)].astype(F32), own)
        proj[pl.ds(pl.multiple_of(i * group, group), group), :] = value.astype(BF16)

    eye = jnp.where(
        lax.broadcasted_iota(jnp.int32, (L, L), 0) == lax.broadcasted_iota(jnp.int32, (L, L), 1),
        1.0,
        0.0,
    ).astype(BF16)
    proj_t = dot_nt(eye, proj[...]).astype(BF16)
    sum_t = dot(proj_t, oht[...])
    z_lane = lax.broadcasted_iota(jnp.int32, sum_t.shape, 1) % 16
    sum_t = (sum_t * jnp.where(z_lane < 8, o0, o1)).astype(BF16).astype(F32)
    f0 = jnp.transpose(sum_t).astype(BF16).reshape(8, 8, 16, L)
    fpad[1:9, 1:9] = f0
    halo_start(fpad, f_s, f_r)

    f_t = sum_t[:C]
    z_own = z_lane[:C]
    stack = jnp.concatenate(
        [
            jnp.where(z_own == 0, 0.0, pltpu.roll(f_t, 1, 1)),
            f_t,
            jnp.where(z_own == 15, 0.0, pltpu.roll(f_t, NV - 1, 1)),
        ],
        axis=0,
    ).astype(BF16)
    for ab in range(9):
        a, b = ab // 3, ab % 3
        window = gpad[2 - a : 10 - a, 2 - b : 10 - b].reshape(NV, L)
        wg[:, ab * L : (ab + 1) * L] = dot(stack, window)

    def tap_block(tap):
        ab, c = tap // 3, tap % 3
        return wg[c * C : (c + 1) * C, ab * L : (ab + 1) * L]

    lane = lax.broadcasted_iota(jnp.int32, (C, L), 1)
    for g in range(7):
        last = tap_block(4 * g + 3) if g < 6 else jnp.zeros((C, L), F32)
        for j in range(3):
            extra = pltpu.roll(last, C - 32 * j, 1)
            block = jnp.where(lane < C, tap_block(4 * g + j), extra)
            pk[9 * g + 3 * j : 9 * g + 3 * j + 3] = block.astype(BF16).reshape(3, CAP, L)
    pk[63] = jnp.zeros((CAP, L), BF16)

    sub = half // plane
    sibling = (gx, gy + 1 - 2 * core)

    def plane_peer(peer):
        return (zi * pz + peer // lanes, lax.rem(peer, lanes) * 2 + core)

    pair = pltpu.make_async_remote_copy(
        src_ref=pk.at[pl.ds((1 - core) * half, half)],
        dst_ref=pair_buf,
        send_sem=pair_s,
        recv_sem=pair_r,
        device_id=sibling,
        device_id_type=MESH,
    )
    pair.start()
    pair.wait_recv()
    both = pk[pl.ds(core * half, half)].astype(F32) + pair_buf[...].astype(F32)
    rs_src[...] = both.astype(BF16)

    @pl.loop(1, plane)
    def _(k):
        peer = lax.rem(slot + k, plane)
        pltpu.make_async_remote_copy(
            src_ref=rs_src.at[pl.ds(peer * sub, sub)],
            dst_ref=rs_buf.at[slot],
            send_sem=rs_s,
            recv_sem=rs_r,
            device_id=plane_peer(peer),
            device_id_type=MESH,
        ).start()

    rs_buf[slot] = rs_src[pl.ds(slot * sub, sub)]
    exchange(rows_d, got_d, d_s, d_r)
    got_d[gx] = rows_d[gx]

    halo_wait(fpad, f_s, f_r)

    @pl.loop(0, 8 // step)
    def _(i):
        windows = [
            fpad[pl.ds(i * step + a, step), b : b + 8].reshape(step * L, L)
            for a in range(3)
            for b in range(3)
        ]
        z3 = dot(jnp.concatenate(windows, axis=1), wf[...])
        out = lift(z3[:, L : 2 * L], z3[:, :L], z3[:, 2 * L :])
        field_y[pl.ds(pl.multiple_of(i * step * L, step * L), step * L), :] = out.astype(BF16)

    whole(rs_buf, plane - 1, rs_s, rs_r).wait_recv()
    total = rs_buf[0].astype(F32)
    for k in range(1, plane):
        total = total + rs_buf[k].astype(F32)
    z_buf[zi] = total.astype(BF16)

    @pl.loop(1, nz)
    def _(k):
        peer = lax.rem(zi + k, nz)
        pltpu.make_async_remote_copy(
            src_ref=z_buf.at[zi],
            dst_ref=z_buf.at[zi],
            send_sem=z_s,
            recv_sem=z_r,
            device_id=(peer * pz + xy, gy),
            device_id_type=MESH,
        ).start()

    @pl.loop(0, groups)
    def _(i):
        base = base_of(i)
        gather(field_y, rows_y, base)

    exchange(rows_y, got_y, y_s, y_r)
    got_y[gx] = rows_y[gx]

    whole(z_buf, nz - 1, z_s, z_r).wait_recv()
    total = z_buf[0].astype(F32)
    for k in range(1, nz):
        total = total + z_buf[k].astype(F32)
    mine = ag_buf.at[core]
    mine[slot] = total.astype(BF16)

    @pl.loop(1, plane)
    def _(k):
        peer = lax.rem(slot + k, plane)
        pltpu.make_async_remote_copy(
            src_ref=mine.at[slot],
            dst_ref=mine.at[slot],
            send_sem=ag_s,
            recv_sem=ag_r,
            device_id=plane_peer(peer),
            device_id_type=MESH,
        ).start()

    whole(got_d, ngx - 1, d_s, d_r).wait_recv()

    @pl.loop(0, groups)
    def _(i):
        part = pl.ds(i * own, own)
        value = unpack(got_d[part].astype(F32), own).astype(BF16)
        grad[part] = dot(value, wint[...]).astype(BF16).reshape(own, CAP, L)

    whole(got_y, ngx - 1, y_s, y_r).wait_recv()

    @pl.loop(0, groups)
    def _(i):
        part = pl.ds(i * own, own)
        value = unpack(got_y[part].astype(F32), own).astype(BF16)
        feat[part] = value[:, :C].reshape(own, CAP, C)

    whole(mine, plane - 1, ag_s, ag_r).wait_recv()
    swap = pltpu.make_async_remote_copy(
        src_ref=mine,
        dst_ref=mine,
        send_sem=swap_s,
        recv_sem=swap_r,
        device_id=sibling,
        device_id_type=MESH,
    )
    swap.start()
    swap.wait_recv()

    whole(vox, ngx - 1, vox_s, vox_r).wait_send()
    whole(rows_p, ngx - 1, pts_s, pts_r).wait_send()
    whole(rows_d, ngx - 1, d_s, d_r).wait_send()
    whole(rows_y, ngx - 1, y_s, y_r).wait_send()
    whole(rs_buf, plane - 1, rs_s, rs_r).wait_send()
    whole(z_buf, nz - 1, z_s, z_r).wait_send()
    whole(mine, plane - 1, ag_s, ag_r).wait_send()
    pair.wait_send()
    swap.wait_send()
    halo_sent(gpad, g_s, g_r)
    halo_sent(fpad, f_s, f_r)


def finish(feat, grad, summed, feat_out, grad_out, wgrad_out, wgrad, sem):
    copies = [
        pltpu.make_async_copy(src, dst, sem.at[n])
        for n, (src, dst) in enumerate(((feat, feat_out), (grad, grad_out)))
    ]
    for copy in copies:
        copy.start()
    plane, sub = summed.shape[1:3]
    half = plane * sub
    lane = lax.broadcasted_iota(jnp.int32, (C, L), 1)
    for g in range(7):
        blocks = []
        for j in range(3):
            first = 9 * g + 3 * j
            parts = [
                summed[r // half, r % half // sub, r % sub] for r in range(first, first + 3)
            ]
            blocks.append(jnp.concatenate(parts).astype(F32))
            wgrad[4 * g + j] = blocks[j][:, :C]
        count = 3
        if g < 6:
            last = pltpu.roll(blocks[0], 32, 1)
            for j in (1, 2):
                last = jnp.where(lane >= 32 * j, pltpu.roll(blocks[j], 32 + 32 * j, 1), last)
            wgrad[4 * g + 3] = last[:, :C]
            count = 4
        part = pl.ds(4 * g, count)
        copies.append(pltpu.make_async_copy(wgrad.at[part], wgrad_out.at[part], sem.at[2 + g]))
        copies[-1].start()
    for copy in copies:
        copy.wait()


def on_device(ngx, ngy, pz, points, counts, voxels, occupancy, weight, w_in, cotangent):
    rows = ngx * CAP
    nz = ngx // pz
    plane = pz * (ngy // 2)
    half = SUB // 2
    vmem = pl.BlockSpec(memory_space=pltpu.VMEM)
    place = pl.BlockSpec(memory_space=pl.ANY)
    dma = pltpu.SemaphoreType.DMA
    feat, grad, summed = pl.pallas_call(
        functools.partial(kernel, ngx, ngy, pz),
        out_shape=(
            pltpu.VMEM((ngx, CAP, C), BF16),
            pltpu.VMEM((ngx, CAP, L), BF16),
            pltpu.VMEM((2, plane, half // plane, CAP, L), BF16),
        ),
        in_specs=[place, place, place, pl.BlockSpec(memory_space=pltpu.SMEM), place, place, place],
        out_specs=(vmem, vmem, vmem),
        scratch_shapes=[
            pltpu.VMEM((ngx, CAP, L), BF16),
            pltpu.VMEM((CAP, ngx), jnp.int32),
            pltpu.VMEM((1, ngx), jnp.int32),
            pltpu.VMEM((27, C, C), BF16),
            pltpu.VMEM((8, 8, 16, C), BF16),
            dma((6,)),
            pltpu.VMEM((ngx, PACK, L), BF16),
            pltpu.VMEM((ngx, PACK, L), BF16),
            pltpu.VMEM((ngx, 1, L), jnp.int32),
            pltpu.VMEM((ngx, PACK, L), BF16),
            pltpu.VMEM((ngx, PACK, L), BF16),
            pltpu.VMEM((rows, L), BF16),
            pltpu.VMEM((ngx, 1, L), jnp.int32),
            pltpu.VMEM((ngx, PACK, L), BF16),
            pltpu.VMEM((ngx, PACK, L), BF16),
            pltpu.VMEM((10, 10, 16, L), BF16),
            pltpu.VMEM((10, 10, 16, L), BF16),
            pltpu.VMEM((9 * L, 3 * L), BF16),
            pltpu.VMEM((3 * L, 9 * L), BF16),
            pltpu.VMEM((L, L), BF16),
            pltpu.VMEM((rows, NV), BF16),
            pltpu.VMEM((NV, L), BF16),
            pltpu.VMEM((NV, L), BF16),
            pltpu.VMEM((3 * C, 9 * L), F32),
            pltpu.VMEM((SUB, CAP, L), BF16),
            pltpu.VMEM((half, CAP, L), BF16),
            pltpu.VMEM((half, CAP, L), BF16),
            pltpu.VMEM((plane, half // plane, CAP, L), BF16),
            pltpu.VMEM((nz, half // plane, CAP, L), BF16),
        ]
        + [dma] * 14
        + [dma((8,))] * 4
        + [dma] * 4,
        compiler_params=pltpu.CompilerParams(
            collective_id=0, has_side_effects=True, vmem_limit_bytes=56 * 1024 * 1024
        ),
    )(
        points.reshape(ngx, CAP, L),
        voxels.reshape(ngx, CAP).T,
        counts.reshape(1, ngx),
        occupancy.reshape(2),
        weight,
        w_in.T,
        cotangent,
    )
    return_shape = (
        jax.ShapeDtypeStruct((ngx, CAP, C), BF16),
        jax.ShapeDtypeStruct((ngx, CAP, L), BF16),
        jax.ShapeDtypeStruct((27, C, C), F32),
    )
    feat, grad, wgrad = pl.pallas_call(
        finish,
        out_shape=return_shape,
        in_specs=[vmem, vmem, vmem],
        out_specs=(place, place, place),
        scratch_shapes=[pltpu.VMEM((27, C, C), F32), dma((9,))],
    )(*(pltpu.with_memory_space_constraint(x, pltpu.VMEM) for x in (feat, grad, summed)))
    return feat[None, None], grad[None, None], wgrad


def solution(mesh):
    ngx, ngy = mesh.shape["gx"], mesh.shape["gy"]
    pz = ngx // 8
    placed = (
        P("gy", "gx", None, None, None),
        P("gy", "gx", None),
        P("gy", "gx", None, None),
        P("gx", "gy", None),
        P(),
        P(),
        P("gx", "gy", None, None),
    )
    return jax.shard_map(
        functools.partial(on_device, ngx, ngy, pz),
        mesh=mesh,
        in_specs=placed,
        out_specs=(P("gy", "gx", None, None, None), P("gy", "gx", None, None, None), P()),
        check_vma=False,
    )
```

```python
import functools

import jax
import jax.numpy as jnp
from jax import lax
from jax.experimental import pallas as pl
from jax.experimental.pallas import tpu as pltpu
from jax.sharding import PartitionSpec as P

MESH = pl.DeviceIdType.MESH
F32 = jnp.float32
BF16 = jnp.bfloat16
C = 96
L = 128
CAP = 32
NV = 1024
SUB = 64
PACK = CAP * C // L


def dot(a, b):
    return jnp.dot(a, b, preferred_element_type=F32)


def dot_nt(a, b):
    return lax.dot_general(a, b, (((1,), (1,)), ((), ())), preferred_element_type=F32)


def pack(value, owners):
    tiles = value.reshape(owners, 4, 8, L)
    tail = tiles[:, 3].reshape(owners * 8, L)
    lane = lax.broadcasted_iota(jnp.int32, (owners * 8, L), 1)
    parts = [
        jnp.where(
            lane < C, tiles[:, j].reshape(owners * 8, L), pltpu.roll(tail, C - 32 * j, 1)
        ).reshape(owners, 1, 8, L)
        for j in range(3)
    ]
    return jnp.concatenate(parts, axis=1).reshape(owners, PACK, L)


def unpack(value, owners):
    tiles = value.reshape(owners, 3, 8, L)
    lane = lax.broadcasted_iota(jnp.int32, (owners * 8, L), 1)
    parts = [tiles[:, j].reshape(owners * 8, L) for j in range(3)]
    tail = jnp.zeros((owners * 8, L), value.dtype)
    for j in range(3):
        moved = pltpu.roll(parts[j], 32 + 32 * j, 1)
        tail = jnp.where((lane >= 32 * j) & (lane < 32 * j + 32), moved, tail)
    parts = [jnp.where(lane < C, part, 0.0) for part in parts] + [tail]
    return jnp.concatenate([part.reshape(owners, 1, 8, L) for part in parts], axis=1).reshape(
        owners * CAP, L
    )


def kernel(
    ngx,
    ngy,
    pz,
    pts_in,
    voxels_in,
    counts_in,
    occ,
    weight_in,
    w_in_t,
    cot_in,
    feat,
    grad,
    ag_buf,
    pts,
    voxels_t,
    counts,
    weight,
    cot,
    in_sem,
    got_y,
    got_d,
    vox,
    rows_p,
    got_p,
    acc,
    got_vox,
    rows_d,
    rows_y,
    gpad,
    fpad,
    wf,
    wb,
    wint,
    oht,
    field_d,
    field_y,
    wg,
    pk,
    pair_buf,
    rs_src,
    rs_buf,
    z_buf,
    vox_s,
    vox_r,
    pts_s,
    pts_r,
    d_s,
    d_r,
    y_s,
    y_r,
    rs_s,
    rs_r,
    z_s,
    z_r,
    ag_s,
    ag_r,
    g_s,
    g_r,
    f_s,
    f_r,
    pair_s,
    pair_r,
    swap_s,
    swap_r,
):
    gx = lax.axis_index("gx")
    gy = lax.axis_index("gy")
    nz = ngx // pz
    half = SUB // 2
    lanes = ngy // 2
    plane = pz * lanes
    zi = gx // pz
    xy = lax.rem(gx, pz)
    core = lax.rem(gy, 2)
    slot = xy * lanes + gy // 2
    rows = ngx * CAP

    wint[C:L, :] = jnp.zeros((L - C, L), BF16)
    fetches = [
        pltpu.make_async_copy(src, dst, in_sem.at[n])
        for n, (src, dst) in enumerate(
            (
                (voxels_in, voxels_t),
                (counts_in, counts),
                (cot_in, cot),
                (w_in_t, wint.at[pl.ds(0, C)]),
                (pts_in, pts),
                (weight_in, weight),
            )
        )
    ]
    for fetch in fetches:
        fetch.start()
    gpad[...] = jnp.zeros_like(gpad)
    fpad[...] = jnp.zeros_like(fpad)

    barrier = pltpu.get_barrier_semaphore()

    def greet(px, py):
        pl.semaphore_signal(barrier, inc=1, device_id=(px, py), device_id_type=MESH)

    @pl.loop(1, ngx)
    def _(k):
        greet(lax.rem(gx + k, ngx), gy)

    @pl.loop(0, pz)
    def _(k):
        for m in range(1, ngy):
            greet(zi * pz + k, lax.rem(gy + m, ngy))

    directions = ((1, 0), (-1, 0), (0, 1), (0, -1), (1, 1), (1, -1), (-1, 1), (-1, -1))

    def exists(dx, dy):
        ok = jnp.bool_(True)
        if dx == 1:
            ok = ok & (gx < ngx - 1)
        if dx == -1:
            ok = ok & (gx > 0)
        if dy == 1:
            ok = ok & (gy < ngy - 1)
        if dy == -1:
            ok = ok & (gy > 0)
        return ok

    for dx, dy in directions[4:]:

        @pl.when(exists(dx, dy))
        def _():
            greet(gx + dx, gy + dy)

    fetches[0].wait()
    fetches[1].wait()
    used = jnp.where(
        lax.broadcasted_iota(jnp.int32, (CAP, ngx), 0) < counts[...], voxels_t[...], -32
    ).astype(F32)
    used = jnp.concatenate([used, jnp.zeros((L - CAP, ngx), F32)], axis=0)
    if ngx < L:
        used = jnp.concatenate([used, jnp.zeros((L, L - ngx), F32)], axis=1)
    vox[...] = jnp.transpose(used)[:ngx].astype(jnp.int32).reshape(ngx, 1, L)

    fetches[2].wait()
    o0 = occ[0].astype(F32)
    o1 = occ[1].astype(F32)

    @pl.loop(0, 8)
    def _(x):
        value = cot[x].astype(F32)
        z = lax.broadcasted_iota(jnp.int32, value.shape, 1)
        gpad[x + 1, pl.ds(1, 8), :, pl.ds(0, C)] = (value * jnp.where(z < 8, o0, o1)).astype(BF16)

    group = min(512, rows)
    own = group // CAP
    groups = ngx // own

    fetches[3].wait()
    fetches[4].wait()

    @pl.loop(0, groups)
    def _(i):
        part = pl.ds(i * own, own)
        rows_p[part] = pack(dot_nt(pts[part].reshape(group, L), wint[...]), own).astype(BF16)

    corners = sum(
        (exists(dx, dy).astype(jnp.int32) for dx, dy in directions[4:]), jnp.int32(0)
    )
    pl.semaphore_wait(barrier, (ngx - 1) + pz * (ngy - 1) + corners)

    def exchange(src, dst, send, recv):
        @pl.loop(1, ngx)
        def _(k):
            peer = lax.rem(gx + k, ngx)
            pltpu.make_async_remote_copy(
                src_ref=src.at[peer],
                dst_ref=dst.at[gx],
                send_sem=send,
                recv_sem=recv,
                device_id=(peer, gy),
                device_id_type=MESH,
            ).start()

    def whole(ref, count, send, recv):
        part = ref.at[pl.ds(0, count)]
        return pltpu.make_async_remote_copy(
            src_ref=part,
            dst_ref=part,
            send_sem=send,
            recv_sem=recv,
            device_id=(gx, gy),
            device_id_type=MESH,
        )

    def halo(ref, d, send, recv):
        dx, dy = directions[d]

        def span(delta, edge):
            if delta == 0:
                return pl.ds(1, 8), pl.ds(1, 8)
            return (8, 0) if delta == 1 else (1, 9)

        sx, tx = span(dx, 0)
        sy, ty = span(dy, 0)
        return pltpu.make_async_remote_copy(
            src_ref=ref.at[sx, sy],
            dst_ref=ref.at[tx, ty],
            send_sem=send.at[d],
            recv_sem=recv.at[d],
            device_id=(gx + dx, gy + dy),
            device_id_type=MESH,
        )

    def halo_start(ref, send, recv):
        for d, (dx, dy) in enumerate(directions):

            @pl.when(exists(dx, dy))
            def _():
                halo(ref, d, send, recv).start()

    def halo_wait(ref, send, recv):
        for d, (dx, dy) in enumerate(directions):

            @pl.when(exists(-dx, -dy))
            def _():
                halo(ref, d, send, recv).wait_recv()

    def halo_sent(ref, send, recv):
        for d, (dx, dy) in enumerate(directions):

            @pl.when(exists(dx, dy))
            def _():
                halo(ref, d, send, recv).wait_send()

    exchange(vox, got_vox, vox_s, vox_r)
    halo_start(gpad, g_s, g_r)
    exchange(rows_p, got_p, pts_s, pts_r.at[gx // own])
    got_vox[gx] = vox[gx]
    got_p[gx] = rows_p[gx]

    fetches[5].wait()
    wf[...] = jnp.zeros_like(wf)
    wb[...] = jnp.zeros_like(wb)
    for tap in range(27):
        ab, c = tap // 3, tap % 3
        value = weight[tap]
        wf[ab * L : ab * L + C, c * L : c * L + C] = value
        wb[c * L : c * L + C, ab * L : ab * L + C] = value

    def lift(total, lower, upper):
        count = total.shape[0]
        z = lax.broadcasted_iota(jnp.int32, total.shape, 0) % 16
        down = pltpu.roll(lower, 1, 0)
        up = pltpu.roll(upper, count - 1, 0)
        total = total + jnp.where(z == 0, 0.0, down) + jnp.where(z == 15, 0.0, up)
        return total * jnp.where(z < 8, o0, o1)

    step = 4

    halo_wait(gpad, g_s, g_r)

    @pl.loop(0, 8 // step)
    def _(i):
        windows = [
            gpad[pl.ds(i * step + 2 - a, step), 2 - b : 10 - b].reshape(step * L, L)
            for a in range(3)
            for b in range(3)
        ]
        z3 = dot_nt(jnp.concatenate(windows, axis=1), wb[...])
        out = lift(z3[:, L : 2 * L], z3[:, 2 * L :], z3[:, :L])
        field_d[pl.ds(pl.multiple_of(i * step * L, step * L), step * L), :] = out.astype(BF16)

    whole(got_vox, ngx - 1, vox_s, vox_r).wait_recv()
    chunk = min(256, rows)
    ids = got_vox[...].reshape(ngx, L)
    high = (ids >> 5).astype(F32).astype(BF16)
    low = (ids & 31).astype(F32).astype(BF16)
    ones = jnp.ones((L, L), BF16)

    @pl.loop(0, rows // chunk)
    def _(i):
        owner = lax.broadcasted_iota(jnp.int32, (chunk, ngx), 0) // CAP + i * (chunk // CAP)
        pick = jnp.where(
            owner == lax.broadcasted_iota(jnp.int32, (chunk, ngx), 1), 1.0, 0.0
        ).astype(BF16)
        here = (
            lax.broadcasted_iota(jnp.int32, (chunk, L), 0) % CAP
            == lax.broadcasted_iota(jnp.int32, (chunk, L), 1)
        )
        hi = jnp.where(here, dot(pick, high) * 32.0, 0.0).astype(BF16)
        lo = jnp.where(here, dot(pick, low), 0.0).astype(BF16)
        wanted = dot(hi, ones) + dot(lo, ones)
        lane = lax.broadcasted_iota(jnp.int32, (chunk, L), 1).astype(F32)
        for j in range(NV // L):
            oht[pl.ds(pl.multiple_of(i * chunk, chunk), chunk), j * L : (j + 1) * L] = jnp.where(
                wanted == lane + float(j * L), 1.0, 0.0
            ).astype(BF16)

    def gather(field, out, base):
        at = pl.ds(pl.multiple_of(base * CAP, group), group)
        out[pl.ds(base, own)] = pack(dot(oht[at, :], field[...]), own).astype(BF16)

    @pl.loop(0, groups)
    def _(i):
        gather(field_d, rows_d, i * own)


    eye = jnp.where(
        lax.broadcasted_iota(jnp.int32, (L, L), 0) == lax.broadcasted_iota(jnp.int32, (L, L), 1),
        1.0,
        0.0,
    ).astype(BF16)

    for i in range(1, groups + 1):
        source = lax.rem(gx // own + groups - i, groups)
        expected = own if i < groups else own - 1
        whole(got_p, expected, pts_s, pts_r.at[source]).wait_recv()
        part = pl.ds(source * own, own)
        at = pl.ds(pl.multiple_of(source * group, group), group)
        value = unpack(got_p[part].astype(F32), own).astype(BF16)
        added = dot(dot_nt(eye, value).astype(BF16), oht[at, :])
        acc[...] = added if i == 1 else acc[...] + added

    sum_t = acc[...]
    z_lane = lax.broadcasted_iota(jnp.int32, sum_t.shape, 1) % 16
    sum_t = (sum_t * jnp.where(z_lane < 8, o0, o1)).astype(BF16).astype(F32)
    f0 = jnp.transpose(sum_t).astype(BF16).reshape(8, 8, 16, L)
    fpad[1:9, 1:9] = f0
    halo_start(fpad, f_s, f_r)

    f_t = sum_t[:C]
    z_own = z_lane[:C]
    stack = jnp.concatenate(
        [
            jnp.where(z_own == 0, 0.0, pltpu.roll(f_t, 1, 1)),
            f_t,
            jnp.where(z_own == 15, 0.0, pltpu.roll(f_t, NV - 1, 1)),
        ],
        axis=0,
    ).astype(BF16)
    for ab in range(9):
        a, b = ab // 3, ab % 3
        window = gpad[2 - a : 10 - a, 2 - b : 10 - b].reshape(NV, L)
        wg[:, ab * L : (ab + 1) * L] = dot(stack, window)

    def tap_block(tap):
        ab, c = tap // 3, tap % 3
        return wg[c * C : (c + 1) * C, ab * L : (ab + 1) * L]

    lane = lax.broadcasted_iota(jnp.int32, (C, L), 1)
    for g in range(7):
        last = tap_block(4 * g + 3) if g < 6 else jnp.zeros((C, L), F32)
        for j in range(3):
            extra = pltpu.roll(last, C - 32 * j, 1)
            block = jnp.where(lane < C, tap_block(4 * g + j), extra)
            pk[9 * g + 3 * j : 9 * g + 3 * j + 3] = block.astype(BF16).reshape(3, CAP, L)
    pk[63] = jnp.zeros((CAP, L), BF16)

    sub = half // plane
    sibling = (gx, gy + 1 - 2 * core)

    def plane_peer(peer):
        return (zi * pz + peer // lanes, lax.rem(peer, lanes) * 2 + core)

    pair = pltpu.make_async_remote_copy(
        src_ref=pk.at[pl.ds((1 - core) * half, half)],
        dst_ref=pair_buf,
        send_sem=pair_s,
        recv_sem=pair_r,
        device_id=sibling,
        device_id_type=MESH,
    )
    pair.start()
    pair.wait_recv()
    both = pk[pl.ds(core * half, half)].astype(F32) + pair_buf[...].astype(F32)
    rs_src[...] = both.astype(BF16)

    @pl.loop(1, plane)
    def _(k):
        peer = lax.rem(slot + k, plane)
        pltpu.make_async_remote_copy(
            src_ref=rs_src.at[pl.ds(peer * sub, sub)],
            dst_ref=rs_buf.at[slot],
            send_sem=rs_s,
            recv_sem=rs_r,
            device_id=plane_peer(peer),
            device_id_type=MESH,
        ).start()

    rs_buf[slot] = rs_src[pl.ds(slot * sub, sub)]
    exchange(rows_d, got_d, d_s, d_r)
    got_d[gx] = rows_d[gx]

    halo_wait(fpad, f_s, f_r)

    @pl.loop(0, 8 // step)
    def _(i):
        windows = [
            fpad[pl.ds(i * step + a, step), b : b + 8].reshape(step * L, L)
            for a in range(3)
            for b in range(3)
        ]
        z3 = dot(jnp.concatenate(windows, axis=1), wf[...])
        out = lift(z3[:, L : 2 * L], z3[:, :L], z3[:, 2 * L :])
        field_y[pl.ds(pl.multiple_of(i * step * L, step * L), step * L), :] = out.astype(BF16)

    whole(rs_buf, plane - 1, rs_s, rs_r).wait_recv()
    total = rs_buf[0].astype(F32)
    for k in range(1, plane):
        total = total + rs_buf[k].astype(F32)
    z_buf[zi] = total.astype(BF16)

    @pl.loop(1, nz)
    def _(k):
        peer = lax.rem(zi + k, nz)
        pltpu.make_async_remote_copy(
            src_ref=z_buf.at[zi],
            dst_ref=z_buf.at[zi],
            send_sem=z_s,
            recv_sem=z_r,
            device_id=(peer * pz + xy, gy),
            device_id_type=MESH,
        ).start()

    @pl.loop(0, groups)
    def _(i):
        gather(field_y, rows_y, i * own)

    exchange(rows_y, got_y, y_s, y_r)
    got_y[gx] = rows_y[gx]

    whole(z_buf, nz - 1, z_s, z_r).wait_recv()
    total = z_buf[0].astype(F32)
    for k in range(1, nz):
        total = total + z_buf[k].astype(F32)
    mine = ag_buf.at[core]
    mine[slot] = total.astype(BF16)

    @pl.loop(1, plane)
    def _(k):
        peer = lax.rem(slot + k, plane)
        pltpu.make_async_remote_copy(
            src_ref=mine.at[slot],
            dst_ref=mine.at[slot],
            send_sem=ag_s,
            recv_sem=ag_r,
            device_id=plane_peer(peer),
            device_id_type=MESH,
        ).start()

    whole(got_d, ngx - 1, d_s, d_r).wait_recv()

    @pl.loop(0, groups)
    def _(i):
        part = pl.ds(i * own, own)
        value = unpack(got_d[part].astype(F32), own).astype(BF16)
        grad[part] = dot(value, wint[...]).astype(BF16).reshape(own, CAP, L)

    whole(got_y, ngx - 1, y_s, y_r).wait_recv()

    @pl.loop(0, groups)
    def _(i):
        part = pl.ds(i * own, own)
        value = unpack(got_y[part].astype(F32), own).astype(BF16)
        feat[part] = value[:, :C].reshape(own, CAP, C)

    whole(mine, plane - 1, ag_s, ag_r).wait_recv()
    swap = pltpu.make_async_remote_copy(
        src_ref=mine,
        dst_ref=mine,
        send_sem=swap_s,
        recv_sem=swap_r,
        device_id=sibling,
        device_id_type=MESH,
    )
    swap.start()
    swap.wait_recv()

    whole(vox, ngx - 1, vox_s, vox_r).wait_send()
    whole(rows_p, ngx - 1, pts_s, pts_r.at[0]).wait_send()
    whole(rows_d, ngx - 1, d_s, d_r).wait_send()
    whole(rows_y, ngx - 1, y_s, y_r).wait_send()
    whole(rs_buf, plane - 1, rs_s, rs_r).wait_send()
    whole(z_buf, nz - 1, z_s, z_r).wait_send()
    whole(mine, plane - 1, ag_s, ag_r).wait_send()
    pair.wait_send()
    swap.wait_send()
    halo_sent(gpad, g_s, g_r)
    halo_sent(fpad, f_s, f_r)


def finish(feat, grad, summed, feat_out, grad_out, wgrad_out, wgrad, sem):
    copies = [
        pltpu.make_async_copy(src, dst, sem.at[n])
        for n, (src, dst) in enumerate(((feat, feat_out), (grad, grad_out)))
    ]
    for copy in copies:
        copy.start()
    plane, sub = summed.shape[1:3]
    half = plane * sub
    lane = lax.broadcasted_iota(jnp.int32, (C, L), 1)
    for g in range(7):
        blocks = []
        for j in range(3):
            first = 9 * g + 3 * j
            parts = [
                summed[r // half, r % half // sub, r % sub] for r in range(first, first + 3)
            ]
            blocks.append(jnp.concatenate(parts).astype(F32))
            wgrad[4 * g + j] = blocks[j][:, :C]
        count = 3
        if g < 6:
            last = pltpu.roll(blocks[0], 32, 1)
            for j in (1, 2):
                last = jnp.where(lane >= 32 * j, pltpu.roll(blocks[j], 32 + 32 * j, 1), last)
            wgrad[4 * g + 3] = last[:, :C]
            count = 4
        part = pl.ds(4 * g, count)
        copies.append(pltpu.make_async_copy(wgrad.at[part], wgrad_out.at[part], sem.at[2 + g]))
        copies[-1].start()
    for copy in copies:
        copy.wait()


def on_device(ngx, ngy, pz, points, counts, voxels, occupancy, weight, w_in, cotangent):
    rows = ngx * CAP
    nz = ngx // pz
    plane = pz * (ngy // 2)
    half = SUB // 2
    vmem = pl.BlockSpec(memory_space=pltpu.VMEM)
    place = pl.BlockSpec(memory_space=pl.ANY)
    dma = pltpu.SemaphoreType.DMA
    feat, grad, summed = pl.pallas_call(
        functools.partial(kernel, ngx, ngy, pz),
        out_shape=(
            pltpu.VMEM((ngx, CAP, C), BF16),
            pltpu.VMEM((ngx, CAP, L), BF16),
            pltpu.VMEM((2, plane, half // plane, CAP, L), BF16),
        ),
        in_specs=[place, place, place, pl.BlockSpec(memory_space=pltpu.SMEM), place, place, place],
        out_specs=(vmem, vmem, vmem),
        scratch_shapes=[
            pltpu.VMEM((ngx, CAP, L), BF16),
            pltpu.VMEM((CAP, ngx), jnp.int32),
            pltpu.VMEM((1, ngx), jnp.int32),
            pltpu.VMEM((27, C, C), BF16),
            pltpu.VMEM((8, 8, 16, C), BF16),
            dma((6,)),
            pltpu.VMEM((ngx, PACK, L), BF16),
            pltpu.VMEM((ngx, PACK, L), BF16),
            pltpu.VMEM((ngx, 1, L), jnp.int32),
            pltpu.VMEM((ngx, PACK, L), BF16),
            pltpu.VMEM((ngx, PACK, L), BF16),
            pltpu.VMEM((L, NV), F32),
            pltpu.VMEM((ngx, 1, L), jnp.int32),
            pltpu.VMEM((ngx, PACK, L), BF16),
            pltpu.VMEM((ngx, PACK, L), BF16),
            pltpu.VMEM((10, 10, 16, L), BF16),
            pltpu.VMEM((10, 10, 16, L), BF16),
            pltpu.VMEM((9 * L, 3 * L), BF16),
            pltpu.VMEM((3 * L, 9 * L), BF16),
            pltpu.VMEM((L, L), BF16),
            pltpu.VMEM((rows, NV), BF16),
            pltpu.VMEM((NV, L), BF16),
            pltpu.VMEM((NV, L), BF16),
            pltpu.VMEM((3 * C, 9 * L), F32),
            pltpu.VMEM((SUB, CAP, L), BF16),
            pltpu.VMEM((half, CAP, L), BF16),
            pltpu.VMEM((half, CAP, L), BF16),
            pltpu.VMEM((plane, half // plane, CAP, L), BF16),
            pltpu.VMEM((nz, half // plane, CAP, L), BF16),
        ]
        + [dma] * 3
        + [dma((pl.cdiv(ngx, 16),))]
        + [dma] * 10
        + [dma((8,))] * 4
        + [dma] * 4,
        compiler_params=pltpu.CompilerParams(
            collective_id=0, has_side_effects=True, vmem_limit_bytes=56 * 1024 * 1024
        ),
    )(
        points.reshape(ngx, CAP, L),
        voxels.reshape(ngx, CAP).T,
        counts.reshape(1, ngx),
        occupancy.reshape(2),
        weight,
        w_in.T,
        cotangent,
    )
    return_shape = (
        jax.ShapeDtypeStruct((ngx, CAP, C), BF16),
        jax.ShapeDtypeStruct((ngx, CAP, L), BF16),
        jax.ShapeDtypeStruct((27, C, C), F32),
    )
    feat, grad, wgrad = pl.pallas_call(
        finish,
        out_shape=return_shape,
        in_specs=[vmem, vmem, vmem],
        out_specs=(place, place, place),
        scratch_shapes=[pltpu.VMEM((27, C, C), F32), dma((9,))],
    )(*(pltpu.with_memory_space_constraint(x, pltpu.VMEM) for x in (feat, grad, summed)))
    return feat[None, None], grad[None, None], wgrad


def solution(mesh):
    ngx, ngy = mesh.shape["gx"], mesh.shape["gy"]
    pz = ngx // 8
    placed = (
        P("gy", "gx", None, None, None),
        P("gy", "gx", None),
        P("gy", "gx", None, None),
        P("gx", "gy", None),
        P(),
        P(),
        P("gx", "gy", None, None),
    )
    return jax.shard_map(
        functools.partial(on_device, ngx, ngy, pz),
        mesh=mesh,
        in_specs=placed,
        out_specs=(P("gy", "gx", None, None, None), P("gy", "gx", None, None, None), P()),
        check_vma=False,
    )
```

```python
import functools

import jax
import jax.numpy as jnp
from jax import lax
from jax.experimental import pallas as pl
from jax.experimental.pallas import tpu as pltpu
from jax.sharding import PartitionSpec as P

MESH = pl.DeviceIdType.MESH
F32 = jnp.float32
BF16 = jnp.bfloat16
C = 96
L = 128
CAP = 32
NV = 1024
SUB = 64
PACK = CAP * C // L


def dot(a, b):
    return jnp.dot(a, b, preferred_element_type=F32)


def dot_nt(a, b):
    return lax.dot_general(a, b, (((1,), (1,)), ((), ())), preferred_element_type=F32)


def pack(value, owners):
    tiles = value.reshape(owners, 4, 8, L)
    tail = tiles[:, 3].reshape(owners * 8, L)
    lane = lax.broadcasted_iota(jnp.int32, (owners * 8, L), 1)
    parts = [
        jnp.where(
            lane < C, tiles[:, j].reshape(owners * 8, L), pltpu.roll(tail, C - 32 * j, 1)
        ).reshape(owners, 1, 8, L)
        for j in range(3)
    ]
    return jnp.concatenate(parts, axis=1).reshape(owners, PACK, L)


def unpack(value, owners):
    tiles = value.reshape(owners, 3, 8, L)
    lane = lax.broadcasted_iota(jnp.int32, (owners * 8, L), 1)
    parts = [tiles[:, j].reshape(owners * 8, L) for j in range(3)]
    tail = jnp.zeros((owners * 8, L), value.dtype)
    for j in range(3):
        moved = pltpu.roll(parts[j], 32 + 32 * j, 1)
        tail = jnp.where((lane >= 32 * j) & (lane < 32 * j + 32), moved, tail)
    parts = [jnp.where(lane < C, part, 0.0) for part in parts] + [tail]
    return jnp.concatenate([part.reshape(owners, 1, 8, L) for part in parts], axis=1).reshape(
        owners * CAP, L
    )


def kernel(
    ngx,
    ngy,
    pz,
    pts_in,
    voxels_in,
    counts_in,
    occ,
    weight_in,
    w_in_t,
    cot_in,
    feat,
    grad,
    ag_buf,
    pts,
    voxels_t,
    counts,
    weight,
    cot,
    in_sem,
    got_y,
    got_d,
    vox,
    rows_p,
    got_p,
    acc,
    got_vox,
    rows_d,
    rows_y,
    gpad,
    fpad,
    wf,
    wb,
    wint,
    oht,
    field_d,
    field_y,
    wg,
    pk,
    pair_buf,
    rs_src,
    rs_buf,
    z_buf,
    vox_s,
    vox_r,
    pts_s,
    pts_r,
    d_s,
    d_r,
    y_s,
    y_r,
    rs_s,
    rs_r,
    z_s,
    z_r,
    ag_s,
    ag_r,
    g_s,
    g_r,
    f_s,
    f_r,
    pair_s,
    pair_r,
    swap_s,
    swap_r,
):
    gx = lax.axis_index("gx")
    gy = lax.axis_index("gy")
    nz = ngx // pz
    half = SUB // 2
    lanes = ngy // 2
    plane = pz * lanes
    zi = gx // pz
    xy = lax.rem(gx, pz)
    core = lax.rem(gy, 2)
    slot = xy * lanes + gy // 2
    rows = ngx * CAP

    wint[C:L, :] = jnp.zeros((L - C, L), BF16)
    fetches = [
        pltpu.make_async_copy(src, dst, in_sem.at[n])
        for n, (src, dst) in enumerate(
            (
                (voxels_in, voxels_t),
                (counts_in, counts),
                (cot_in, cot),
                (w_in_t, wint.at[pl.ds(0, C)]),
                (pts_in, pts),
                (weight_in, weight),
            )
        )
    ]
    for fetch in fetches:
        fetch.start()
    gpad[...] = jnp.zeros_like(gpad)
    fpad[...] = jnp.zeros_like(fpad)

    barrier = pltpu.get_barrier_semaphore()

    def greet(px, py):
        pl.semaphore_signal(barrier, inc=1, device_id=(px, py), device_id_type=MESH)

    @pl.loop(1, ngx)
    def _(k):
        greet(lax.rem(gx + k, ngx), gy)

    @pl.loop(0, pz)
    def _(k):
        for m in range(1, ngy):
            greet(zi * pz + k, lax.rem(gy + m, ngy))

    directions = ((1, 0), (-1, 0), (0, 1), (0, -1), (1, 1), (1, -1), (-1, 1), (-1, -1))

    def exists(dx, dy):
        ok = jnp.bool_(True)
        if dx == 1:
            ok = ok & (gx < ngx - 1)
        if dx == -1:
            ok = ok & (gx > 0)
        if dy == 1:
            ok = ok & (gy < ngy - 1)
        if dy == -1:
            ok = ok & (gy > 0)
        return ok

    for dx, dy in directions[4:]:

        @pl.when(exists(dx, dy))
        def _():
            greet(gx + dx, gy + dy)

    fetches[0].wait()
    fetches[1].wait()
    used = jnp.where(
        lax.broadcasted_iota(jnp.int32, (CAP, ngx), 0) < counts[...], voxels_t[...], -32
    ).astype(F32)
    used = jnp.concatenate([used, jnp.zeros((L - CAP, ngx), F32)], axis=0)
    if ngx < L:
        used = jnp.concatenate([used, jnp.zeros((L, L - ngx), F32)], axis=1)
    vox[...] = jnp.transpose(used)[:ngx].astype(jnp.int32).reshape(ngx, 1, L)

    fetches[2].wait()
    o0 = occ[0].astype(F32)
    o1 = occ[1].astype(F32)

    @pl.loop(0, 8)
    def _(x):
        value = cot[x].astype(F32)
        z = lax.broadcasted_iota(jnp.int32, value.shape, 1)
        gpad[x + 1, pl.ds(1, 8), :, pl.ds(0, C)] = (value * jnp.where(z < 8, o0, o1)).astype(BF16)

    corners = sum(
        (exists(dx, dy).astype(jnp.int32) for dx, dy in directions[4:]), jnp.int32(0)
    )
    pl.semaphore_wait(barrier, (ngx - 1) + pz * (ngy - 1) + corners)

    group = min(512, rows)
    own = group // CAP
    groups = ngx // own

    def base_of(i):
        return lax.rem(gx // own + i, groups) * own

    def exchange_group(src, dst, send, recv, base):
        @pl.loop(0, own)
        def _(k):
            peer = base + lax.rem(gx + k, own)

            @pl.when(peer != gx)
            def _():
                pltpu.make_async_remote_copy(
                    src_ref=src.at[peer],
                    dst_ref=dst.at[gx],
                    send_sem=send,
                    recv_sem=recv,
                    device_id=(peer, gy),
                    device_id_type=MESH,
                ).start()

    def exchange(src, dst, send, recv):
        @pl.loop(1, ngx)
        def _(k):
            peer = lax.rem(gx + k, ngx)
            pltpu.make_async_remote_copy(
                src_ref=src.at[peer],
                dst_ref=dst.at[gx],
                send_sem=send,
                recv_sem=recv,
                device_id=(peer, gy),
                device_id_type=MESH,
            ).start()

    def whole(ref, count, send, recv):
        part = ref.at[pl.ds(0, count)]
        return pltpu.make_async_remote_copy(
            src_ref=part,
            dst_ref=part,
            send_sem=send,
            recv_sem=recv,
            device_id=(gx, gy),
            device_id_type=MESH,
        )

    def halo(ref, d, send, recv):
        dx, dy = directions[d]

        def span(delta, edge):
            if delta == 0:
                return pl.ds(1, 8), pl.ds(1, 8)
            return (8, 0) if delta == 1 else (1, 9)

        sx, tx = span(dx, 0)
        sy, ty = span(dy, 0)
        return pltpu.make_async_remote_copy(
            src_ref=ref.at[sx, sy],
            dst_ref=ref.at[tx, ty],
            send_sem=send.at[d],
            recv_sem=recv.at[d],
            device_id=(gx + dx, gy + dy),
            device_id_type=MESH,
        )

    def halo_start(ref, send, recv):
        for d, (dx, dy) in enumerate(directions):

            @pl.when(exists(dx, dy))
            def _():
                halo(ref, d, send, recv).start()

    def halo_wait(ref, send, recv):
        for d, (dx, dy) in enumerate(directions):

            @pl.when(exists(-dx, -dy))
            def _():
                halo(ref, d, send, recv).wait_recv()

    def halo_sent(ref, send, recv):
        for d, (dx, dy) in enumerate(directions):

            @pl.when(exists(dx, dy))
            def _():
                halo(ref, d, send, recv).wait_send()

    exchange(vox, got_vox, vox_s, vox_r)
    halo_start(gpad, g_s, g_r)
    fetches[3].wait()
    fetches[4].wait()

    @pl.loop(0, groups)
    def _(i):
        base = base_of(i)
        part = pl.ds(base, own)
        rows_p[part] = pack(dot_nt(pts[part].reshape(group, L), wint[...]), own).astype(BF16)

    exchange(rows_p, got_p, pts_s, pts_r.at[gx // own])
    got_vox[gx] = vox[gx]
    got_p[gx] = rows_p[gx]

    fetches[5].wait()
    wf[...] = jnp.zeros_like(wf)
    wb[...] = jnp.zeros_like(wb)
    for tap in range(27):
        ab, c = tap // 3, tap % 3
        value = weight[tap]
        wf[ab * L : ab * L + C, c * L : c * L + C] = value
        wb[c * L : c * L + C, ab * L : ab * L + C] = value

    def lift(total, lower, upper):
        count = total.shape[0]
        z = lax.broadcasted_iota(jnp.int32, total.shape, 0) % 16
        down = pltpu.roll(lower, 1, 0)
        up = pltpu.roll(upper, count - 1, 0)
        total = total + jnp.where(z == 0, 0.0, down) + jnp.where(z == 15, 0.0, up)
        return total * jnp.where(z < 8, o0, o1)

    step = 4

    halo_wait(gpad, g_s, g_r)

    @pl.loop(0, 8 // step)
    def _(i):
        windows = [
            gpad[pl.ds(i * step + 2 - a, step), 2 - b : 10 - b].reshape(step * L, L)
            for a in range(3)
            for b in range(3)
        ]
        z3 = dot_nt(jnp.concatenate(windows, axis=1), wb[...])
        out = lift(z3[:, L : 2 * L], z3[:, 2 * L :], z3[:, :L])
        field_d[pl.ds(pl.multiple_of(i * step * L, step * L), step * L), :] = out.astype(BF16)

    whole(got_vox, ngx - 1, vox_s, vox_r).wait_recv()
    chunk = min(512, rows)
    ids = got_vox[...].reshape(ngx, L)
    low = pltpu.roll((ids & 31).astype(F32), CAP, 1)
    digits = ((ids >> 5).astype(F32) + low).astype(BF16)
    ones = jnp.ones((L, L), BF16)

    @pl.loop(0, rows // chunk)
    def _(i):
        owner = lax.broadcasted_iota(jnp.int32, (chunk, ngx), 0) // CAP + i * (chunk // CAP)
        pick = jnp.where(
            owner == lax.broadcasted_iota(jnp.int32, (chunk, ngx), 1), 1.0, 0.0
        ).astype(BF16)
        place = lax.broadcasted_iota(jnp.int32, (chunk, L), 0) % CAP
        column = lax.broadcasted_iota(jnp.int32, (chunk, L), 1)
        both = dot(pick, digits)
        both = jnp.where(
            column == place, both * 32.0, jnp.where(column == place + CAP, both, 0.0)
        )
        wanted = dot(both.astype(BF16), ones)
        lane = lax.broadcasted_iota(jnp.int32, (chunk, L), 1).astype(F32)
        for j in range(NV // L):
            oht[pl.ds(pl.multiple_of(i * chunk, chunk), chunk), j * L : (j + 1) * L] = jnp.where(
                wanted == lane + float(j * L), 1.0, 0.0
            ).astype(BF16)

    def gather(field, out, base):
        at = pl.ds(pl.multiple_of(base * CAP, group), group)
        out[pl.ds(base, own)] = pack(dot(oht[at, :], field[...]), own).astype(BF16)

    @pl.loop(0, groups)
    def _(i):
        gather(field_d, rows_d, i * own)


    eye = jnp.where(
        lax.broadcasted_iota(jnp.int32, (L, L), 0) == lax.broadcasted_iota(jnp.int32, (L, L), 1),
        1.0,
        0.0,
    ).astype(BF16)

    for i in range(1, groups + 1):
        source = lax.rem(gx // own + groups - i, groups)
        expected = own if i < groups else own - 1
        whole(got_p, expected, pts_s, pts_r.at[source]).wait_recv()
        part = pl.ds(source * own, own)
        at = pl.ds(pl.multiple_of(source * group, group), group)
        value = unpack(got_p[part].astype(F32), own).astype(BF16)
        added = dot(dot_nt(eye, value).astype(BF16), oht[at, :])
        acc[...] = added if i == 1 else acc[...] + added

    sum_t = acc[...]
    z_lane = lax.broadcasted_iota(jnp.int32, sum_t.shape, 1) % 16
    sum_t = (sum_t * jnp.where(z_lane < 8, o0, o1)).astype(BF16).astype(F32)
    f0 = jnp.transpose(sum_t).astype(BF16).reshape(8, 8, 16, L)
    fpad[1:9, 1:9] = f0
    halo_start(fpad, f_s, f_r)

    f_t = sum_t[:C]
    z_own = z_lane[:C]
    stack = jnp.concatenate(
        [
            jnp.where(z_own == 0, 0.0, pltpu.roll(f_t, 1, 1)),
            f_t,
            jnp.where(z_own == 15, 0.0, pltpu.roll(f_t, NV - 1, 1)),
        ],
        axis=0,
    ).astype(BF16)
    for ab in range(9):
        a, b = ab // 3, ab % 3
        window = gpad[2 - a : 10 - a, 2 - b : 10 - b].reshape(NV, L)
        wg[:, ab * L : (ab + 1) * L] = dot(stack, window)

    def tap_block(tap):
        ab, c = tap // 3, tap % 3
        return wg[c * C : (c + 1) * C, ab * L : (ab + 1) * L]

    lane = lax.broadcasted_iota(jnp.int32, (C, L), 1)
    for g in range(7):
        last = tap_block(4 * g + 3) if g < 6 else jnp.zeros((C, L), F32)
        for j in range(3):
            extra = pltpu.roll(last, C - 32 * j, 1)
            block = jnp.where(lane < C, tap_block(4 * g + j), extra)
            pk[9 * g + 3 * j : 9 * g + 3 * j + 3] = block.astype(BF16).reshape(3, CAP, L)
    pk[63] = jnp.zeros((CAP, L), BF16)

    sub = half // plane
    sibling = (gx, gy + 1 - 2 * core)

    def plane_peer(peer):
        return (zi * pz + peer // lanes, lax.rem(peer, lanes) * 2 + core)

    pair = pltpu.make_async_remote_copy(
        src_ref=pk.at[pl.ds((1 - core) * half, half)],
        dst_ref=pair_buf,
        send_sem=pair_s,
        recv_sem=pair_r,
        device_id=sibling,
        device_id_type=MESH,
    )
    pair.start()
    pair.wait_recv()
    both = pk[pl.ds(core * half, half)].astype(F32) + pair_buf[...].astype(F32)
    rs_src[...] = both.astype(BF16)

    @pl.loop(1, plane)
    def _(k):
        peer = lax.rem(slot + k, plane)
        pltpu.make_async_remote_copy(
            src_ref=rs_src.at[pl.ds(peer * sub, sub)],
            dst_ref=rs_buf.at[slot],
            send_sem=rs_s,
            recv_sem=rs_r,
            device_id=plane_peer(peer),
            device_id_type=MESH,
        ).start()

    rs_buf[slot] = rs_src[pl.ds(slot * sub, sub)]
    exchange(rows_d, got_d, d_s, d_r)
    got_d[gx] = rows_d[gx]

    halo_wait(fpad, f_s, f_r)

    @pl.loop(0, 8 // step)
    def _(i):
        windows = [
            fpad[pl.ds(i * step + a, step), b : b + 8].reshape(step * L, L)
            for a in range(3)
            for b in range(3)
        ]
        z3 = dot(jnp.concatenate(windows, axis=1), wf[...])
        out = lift(z3[:, L : 2 * L], z3[:, :L], z3[:, 2 * L :])
        field_y[pl.ds(pl.multiple_of(i * step * L, step * L), step * L), :] = out.astype(BF16)

    whole(rs_buf, plane - 1, rs_s, rs_r).wait_recv()
    total = rs_buf[0].astype(F32)
    for k in range(1, plane):
        total = total + rs_buf[k].astype(F32)
    z_buf[zi] = total.astype(BF16)

    @pl.loop(1, nz)
    def _(k):
        peer = lax.rem(zi + k, nz)
        pltpu.make_async_remote_copy(
            src_ref=z_buf.at[zi],
            dst_ref=z_buf.at[zi],
            send_sem=z_s,
            recv_sem=z_r,
            device_id=(peer * pz + xy, gy),
            device_id_type=MESH,
        ).start()

    @pl.loop(0, groups)
    def _(i):
        base = base_of(i)
        gather(field_y, rows_y, base)

    exchange(rows_y, got_y, y_s, y_r)
    got_y[gx] = rows_y[gx]

    whole(z_buf, nz - 1, z_s, z_r).wait_recv()
    total = z_buf[0].astype(F32)
    for k in range(1, nz):
        total = total + z_buf[k].astype(F32)
    mine = ag_buf.at[core]
    mine[slot] = total.astype(BF16)

    @pl.loop(1, plane)
    def _(k):
        peer = lax.rem(slot + k, plane)
        pltpu.make_async_remote_copy(
            src_ref=mine.at[slot],
            dst_ref=mine.at[slot],
            send_sem=ag_s,
            recv_sem=ag_r,
            device_id=plane_peer(peer),
            device_id_type=MESH,
        ).start()

    whole(got_d, ngx - 1, d_s, d_r).wait_recv()

    @pl.loop(0, groups)
    def _(i):
        part = pl.ds(i * own, own)
        value = unpack(got_d[part].astype(F32), own).astype(BF16)
        grad[part] = dot(value, wint[...]).astype(BF16).reshape(own, CAP, L)

    whole(got_y, ngx - 1, y_s, y_r).wait_recv()

    @pl.loop(0, groups)
    def _(i):
        part = pl.ds(i * own, own)
        value = unpack(got_y[part].astype(F32), own).astype(BF16)
        feat[part] = value[:, :C].reshape(own, CAP, C)

    whole(mine, plane - 1, ag_s, ag_r).wait_recv()
    swap = pltpu.make_async_remote_copy(
        src_ref=mine,
        dst_ref=mine,
        send_sem=swap_s,
        recv_sem=swap_r,
        device_id=sibling,
        device_id_type=MESH,
    )
    swap.start()
    swap.wait_recv()

    whole(vox, ngx - 1, vox_s, vox_r).wait_send()
    whole(rows_p, ngx - 1, pts_s, pts_r.at[0]).wait_send()
    whole(rows_d, ngx - 1, d_s, d_r).wait_send()
    whole(rows_y, ngx - 1, y_s, y_r).wait_send()
    whole(rs_buf, plane - 1, rs_s, rs_r).wait_send()
    whole(z_buf, nz - 1, z_s, z_r).wait_send()
    whole(mine, plane - 1, ag_s, ag_r).wait_send()
    pair.wait_send()
    swap.wait_send()
    halo_sent(gpad, g_s, g_r)
    halo_sent(fpad, f_s, f_r)


def finish(feat, grad, summed, feat_out, grad_out, wgrad_out, wgrad, sem):
    copies = [
        pltpu.make_async_copy(src, dst, sem.at[n])
        for n, (src, dst) in enumerate(((feat, feat_out), (grad, grad_out)))
    ]
    for copy in copies:
        copy.start()
    plane, sub = summed.shape[1:3]
    half = plane * sub
    lane = lax.broadcasted_iota(jnp.int32, (C, L), 1)
    for g in range(7):
        blocks = []
        for j in range(3):
            first = 9 * g + 3 * j
            parts = [
                summed[r // half, r % half // sub, r % sub] for r in range(first, first + 3)
            ]
            blocks.append(jnp.concatenate(parts).astype(F32))
            wgrad[4 * g + j] = blocks[j][:, :C]
        count = 3
        if g < 6:
            last = pltpu.roll(blocks[0], 32, 1)
            for j in (1, 2):
                last = jnp.where(lane >= 32 * j, pltpu.roll(blocks[j], 32 + 32 * j, 1), last)
            wgrad[4 * g + 3] = last[:, :C]
            count = 4
        part = pl.ds(4 * g, count)
        copies.append(pltpu.make_async_copy(wgrad.at[part], wgrad_out.at[part], sem.at[2 + g]))
        copies[-1].start()
    for copy in copies:
        copy.wait()


def on_device(ngx, ngy, pz, points, counts, voxels, occupancy, weight, w_in, cotangent):
    rows = ngx * CAP
    nz = ngx // pz
    plane = pz * (ngy // 2)
    half = SUB // 2
    vmem = pl.BlockSpec(memory_space=pltpu.VMEM)
    place = pl.BlockSpec(memory_space=pl.ANY)
    dma = pltpu.SemaphoreType.DMA
    feat, grad, summed = pl.pallas_call(
        functools.partial(kernel, ngx, ngy, pz),
        out_shape=(
            pltpu.VMEM((ngx, CAP, C), BF16),
            pltpu.VMEM((ngx, CAP, L), BF16),
            pltpu.VMEM((2, plane, half // plane, CAP, L), BF16),
        ),
        in_specs=[place, place, place, pl.BlockSpec(memory_space=pltpu.SMEM), place, place, place],
        out_specs=(vmem, vmem, vmem),
        scratch_shapes=[
            pltpu.VMEM((ngx, CAP, L), BF16),
            pltpu.VMEM((CAP, ngx), jnp.int32),
            pltpu.VMEM((1, ngx), jnp.int32),
            pltpu.VMEM((27, C, C), BF16),
            pltpu.VMEM((8, 8, 16, C), BF16),
            dma((6,)),
            pltpu.VMEM((ngx, PACK, L), BF16),
            pltpu.VMEM((ngx, PACK, L), BF16),
            pltpu.VMEM((ngx, 1, L), jnp.int32),
            pltpu.VMEM((ngx, PACK, L), BF16),
            pltpu.VMEM((ngx, PACK, L), BF16),
            pltpu.VMEM((L, NV), F32),
            pltpu.VMEM((ngx, 1, L), jnp.int32),
            pltpu.VMEM((ngx, PACK, L), BF16),
            pltpu.VMEM((ngx, PACK, L), BF16),
            pltpu.VMEM((10, 10, 16, L), BF16),
            pltpu.VMEM((10, 10, 16, L), BF16),
            pltpu.VMEM((9 * L, 3 * L), BF16),
            pltpu.VMEM((3 * L, 9 * L), BF16),
            pltpu.VMEM((L, L), BF16),
            pltpu.VMEM((rows, NV), BF16),
            pltpu.VMEM((NV, L), BF16),
            pltpu.VMEM((NV, L), BF16),
            pltpu.VMEM((3 * C, 9 * L), F32),
            pltpu.VMEM((SUB, CAP, L), BF16),
            pltpu.VMEM((half, CAP, L), BF16),
            pltpu.VMEM((half, CAP, L), BF16),
            pltpu.VMEM((plane, half // plane, CAP, L), BF16),
            pltpu.VMEM((nz, half // plane, CAP, L), BF16),
        ]
        + [dma] * 3
        + [dma((pl.cdiv(ngx, 16),))]
        + [dma] * 10
        + [dma((8,))] * 4
        + [dma] * 4,
        compiler_params=pltpu.CompilerParams(
            collective_id=0, has_side_effects=True, vmem_limit_bytes=56 * 1024 * 1024
        ),
    )(
        points.reshape(ngx, CAP, L),
        voxels.reshape(ngx, CAP).T,
        counts.reshape(1, ngx),
        occupancy.reshape(2),
        weight,
        w_in.T,
        cotangent,
    )
    return_shape = (
        jax.ShapeDtypeStruct((ngx, CAP, C), BF16),
        jax.ShapeDtypeStruct((ngx, CAP, L), BF16),
        jax.ShapeDtypeStruct((27, C, C), F32),
    )
    feat, grad, wgrad = pl.pallas_call(
        finish,
        out_shape=return_shape,
        in_specs=[vmem, vmem, vmem],
        out_specs=(place, place, place),
        scratch_shapes=[pltpu.VMEM((27, C, C), F32), dma((9,))],
    )(*(pltpu.with_memory_space_constraint(x, pltpu.VMEM) for x in (feat, grad, summed)))
    return feat[None, None], grad[None, None], wgrad


def solution(mesh):
    ngx, ngy = mesh.shape["gx"], mesh.shape["gy"]
    pz = ngx // 8
    placed = (
        P("gy", "gx", None, None, None),
        P("gy", "gx", None),
        P("gy", "gx", None, None),
        P("gx", "gy", None),
        P(),
        P(),
        P("gx", "gy", None, None),
    )
    return jax.shard_map(
        functools.partial(on_device, ngx, ngy, pz),
        mesh=mesh,
        in_specs=placed,
        out_specs=(P("gy", "gx", None, None, None), P("gy", "gx", None, None, None), P()),
        check_vma=False,
    )
```
